512 devices in a mesh: tx: 8 (over z_lo), ty: 8 (over y, core), src: 8 (over z_hi, x).
Axes of the slice: x: 4, y: 4, z: 16 (z_hi: 2, z_lo: 8; z = z_hi * 8 + z_lo), core: 2. Of those that a mesh axis runs over, the one named last changes fastest.
Arguments:
- adj_now: float32 [8, 3, 64, 128, 256], P('src', None, 'tx', 'ty'), may hold values from -6 to 6
- adj_later: float32 [8, 3, 64, 128, 256], P('src', None, 'tx', 'ty'), may hold values from -6 to 6
- forward_field: bfloat16 [8, 3, 3, 64, 128, 256], P('src', None, None, 'tx', 'ty'), may hold values from -6 to 6
- lame_first: float32 [64, 128, 256], P('tx', 'ty'), may hold values from 0.5 to 2
- shear: float32 [64, 128, 256], P('tx', 'ty'), may hold values from 0.3 to 1.5
- buoyancy: float32 [64, 128, 256], P('tx', 'ty'), may hold values from 0.5 to 1.5
- seafloor_depth: int32 [64, 128], P('tx', 'ty'), may hold values from 126 to 255
- station_columns: int32 [8, 64], P('src'), may hold values from 0 to 8191
- station_traces: float32 [8, 3, 64], P('src'), may hold values from -60 to 60
Outputs:
- adj_final: float32 [8, 3, 64, 128, 256], P('src', None, 'tx', 'ty')
- kernels: float32 [2, 64, 128, 256], P(None, 'tx', 'ty', 'src')
The draws below stay inside these ranges and needn't reach their ends.
All inputs are finite; a program needn't handle non-finite values.
Results may differ from the reference program's by a relative error of at most 0.0003.
Values may be sent and summed in bfloat16 or wider, within the bound.
A program may use at most 64 MiB of HBM per device.

```python
import math
import jax
import jax.numpy as jnp
from jax import lax

CX = 8
CY = 16
NZ = 256
STEPS = 3
STATIONS = 64
NX = 64
NY = 128
SOURCES = 8


def draw_seafloor_depth(key, part):
    key_tile, key_rough = jax.random.split(jax.random.fold_in(key, 17))
    unit_cells = max(1, NZ // 32)
    levels = jnp.array([1, 2, 4, 8, 16], dtype=jnp.int32)
    picked = jax.random.randint(key_tile, (NX // CX, NY // CY), 0, 5)
    thickness = levels[picked] * unit_cells
    spread_tiles = jnp.repeat(jnp.repeat(thickness, CX, axis=0), CY, axis=1)
    rough = jax.random.randint(key_rough, (NX, NY), 0, 3)
    return (NZ - spread_tiles - rough).astype(jnp.int32)


def set_ends(entries, key, smallest, high):
    extent = entries.shape
    index_at = [jax.random.randint(jax.random.fold_in(key, axis), (), 0, extent[axis]) for axis in range(len(extent))]
    entries = entries.at[tuple(index_at)].set(smallest)
    longest = extent.index(max(extent))
    index_at[longest] = (index_at[longest] + 1) % extent[longest]
    return entries.at[tuple(index_at)].set(high)


def block_scale(own_key, shape, cuts, smallest, top_value):
    level = 1.0
    for dim, blocks in cuts:
        draws = jax.random.uniform(jax.random.fold_in(jax.random.fold_in(own_key, 6), dim), (blocks,), jnp.float32, smallest / len(cuts), top_value / len(cuts))
        level = level * jnp.repeat(jnp.exp(draws), shape[dim] // blocks).reshape((-1,) + (1,) * (len(shape) - 1 - dim))
    return level


def scatter_about(own_key, shape, spread, reach, cuts=(), kind=jnp.bfloat16):
    drawn = spread * jax.random.normal(own_key, shape, jnp.float32)
    if cuts:
        drawn = drawn * block_scale(own_key, shape, cuts, -0.22, 0.18)
    return jnp.clip(drawn, -reach, reach).astype(kind)


def setup_inputs(seed: int = 0) -> dict:
    key_list = jax.random.split(jax.random.key(seed), 10)
    adj_now = scatter_about(key_list[0], (SOURCES, 3, NX, NY, NZ), 1.0, 6.0, ((0, 8), (2, 8), (3, 8)), jnp.float32)
    adj_later = scatter_about(key_list[1], (SOURCES, 3, NX, NY, NZ), 1.0, 6.0, ((0, 8), (2, 8), (3, 8)), jnp.float32)
    forward_field = scatter_about(key_list[2], (SOURCES, STEPS, 3, NX, NY, NZ), 1.0, 6.0, ((0, 8), (3, 8), (4, 8)))
    lame_first = jnp.clip(jnp.exp(math.log(2.0) - 1.3862944 * jax.random.uniform(key_list[3], (NX, NY, NZ), jnp.float32) ** block_scale(key_list[3], (NX, NY, NZ), ((0, 8), (1, 8)), -0.2, 0.2)), 0.5, 2.0)
    shear = jnp.clip(jnp.exp(math.log(1.5) - 1.60943787 * jax.random.uniform(key_list[4], (NX, NY, NZ), jnp.float32) ** block_scale(key_list[4], (NX, NY, NZ), ((0, 8), (1, 8)), -0.2, 0.2)), 0.3, 1.5)
    buoyancy = jnp.clip(jnp.exp(math.log(1.5) - 1.0986123 * jax.random.uniform(key_list[5], (NX, NY, NZ), jnp.float32) ** block_scale(key_list[5], (NX, NY, NZ), ((0, 8), (1, 8)), -0.2, 0.2)), 0.5, 1.5)
    seafloor_depth = draw_seafloor_depth(jax.random.fold_in(key_list[9], 71), 0)
    station_columns = set_ends(jax.random.randint(key_list[7], (SOURCES, STATIONS), 0, NX * NY), jax.random.fold_in(key_list[7], 1), 0, (NX * NY) - 1).astype(jnp.int32)
    station_traces = scatter_about(key_list[8], (SOURCES, STEPS, STATIONS), 10.0, 60.0, ((0, 8),), jnp.float32)
    return dict(adj_now=adj_now, adj_later=adj_later, forward_field=forward_field, lame_first=lame_first, shear=shear, buoyancy=buoyancy, seafloor_depth=seafloor_depth, station_columns=station_columns, station_traces=station_traces)


step_squared = 0.04


def shifted(padded, dx, dy, dz):
    span_x = padded.shape[-3] - 2
    span_y = padded.shape[-2] - 2
    span_z = padded.shape[-1] - 2
    return padded[..., 1 + dx:1 + dx + span_x, 1 + dy:1 + dy + span_y, 1 + dz:1 + dz + span_z]


def unit_axis(k, sign):
    offset = [0, 0, 0]
    offset[k] = sign
    return offset


def pair_offset(k, sk, d, sd):
    offset = [0, 0, 0]
    offset[k] = offset[k] + sk
    offset[d] = offset[d] + sd
    return offset


def depth_pad(field):
    return jnp.pad(field, [(0, 0)] * (field.ndim - 1) + [(1, 1)])


def elastic_force(field, lame, mu_eff, buoy):
    padded = depth_pad(field)
    parts = []
    for k in range(3):
        piece = padded[..., k, :, :, :]
        centre = shifted(piece, 0, 0, 0)
        laplace = -6.0 * centre
        for d in range(3):
            laplace = laplace + shifted(piece, *unit_axis(d, 1)) + shifted(piece, *unit_axis(d, -1))
        grad_div = shifted(piece, *unit_axis(k, 1)) - 2.0 * centre + shifted(piece, *unit_axis(k, -1))
        for d in range(3):
            if d != k:
                other = padded[..., d, :, :, :]
                grad_div = grad_div + 0.25 * (shifted(other, *pair_offset(k, 1, d, 1)) - shifted(other, *pair_offset(k, 1, d, -1)) - shifted(other, *pair_offset(k, -1, d, 1)) + shifted(other, *pair_offset(k, -1, d, -1)))
        parts.append(buoy * (mu_eff * laplace + (lame + mu_eff) * grad_div))
    return jnp.stack(parts, axis=-4)


def gradients(field):
    padded = depth_pad(field)
    table = []
    for k in range(3):
        piece = padded[..., k, :, :, :]
        table.append([0.5 * (shifted(piece, *unit_axis(d, 1)) - shifted(piece, *unit_axis(d, -1))) for d in range(3)])
    return table


def accumulate(kernel_lam, kernel_mu, adj_padded, fwd_padded, solid_mask):
    grad_adj = gradients(adj_padded)
    grad_fwd = gradients(fwd_padded)
    div_adj = grad_adj[0][0] + grad_adj[1][1] + grad_adj[2][2]
    div_fwd = grad_fwd[0][0] + grad_fwd[1][1] + grad_fwd[2][2]
    contraction = grad_adj[0][0] * grad_fwd[0][0]
    for k in range(3):
        for d in range(3):
            if k + d > 0:
                contraction = contraction + grad_adj[k][d] * grad_fwd[k][d]
    kernel_lam = kernel_lam + jnp.sum(div_adj * div_fwd, axis=0)
    kernel_mu = kernel_mu + jnp.sum(solid_mask * contraction, axis=0)
    return kernel_lam, kernel_mu


def vertical_source(columns, amps, depth_region, anchor_x, anchor_y, total_y, depth_cells):
    ext_x, ext_y = depth_region.shape
    loc_x = columns // total_y - anchor_x
    loc_y = columns % total_y - anchor_y
    inside = (loc_x >= 0) & (loc_x < ext_x) & (loc_y >= 0) & (loc_y < ext_y)
    loc_x = jnp.clip(loc_x, 0, ext_x - 1).astype(jnp.int32)
    loc_y = jnp.clip(loc_y, 0, ext_y - 1).astype(jnp.int32)
    cell_z = depth_region[loc_x, loc_y].astype(jnp.int32)
    values = jnp.where(inside, amps, jnp.zeros_like(amps))
    rows = lax.broadcasted_iota(jnp.int32, columns.shape, 0)
    field = jnp.zeros((columns.shape[0], ext_x * ext_y, depth_cells), amps.dtype)
    field = field.at[rows, loc_x * ext_y + loc_y, cell_z].add(values)
    return field.reshape(columns.shape[0], ext_x, ext_y, depth_cells)


def pad_plane(field):
    return jnp.pad(field, ((0, 0), (0, 0), (1, 1), (1, 1), (0, 0)))


def reference(adj_now, adj_later, forward_field, lame_first, shear, buoyancy, seafloor_depth, station_columns, station_traces):
    levels = lax.broadcasted_iota(jnp.int32, (NX, NY, NZ), 2)
    solid_mask = (levels >= seafloor_depth[:, :, None]).astype(lame_first.dtype)
    mu_eff = shear * solid_mask

    def one_source(items):
        adj_cur, adj_prev, forward_one, columns_one, traces_one = items
        adj_cur = adj_cur[None]
        adj_prev = adj_prev[None]
        forward_one = forward_one[None]
        columns_one = columns_one[None]
        traces_one = traces_one[None]
        kernel_lam = jnp.zeros((NX, NY, NZ), jnp.float32)
        kernel_mu = jnp.zeros((NX, NY, NZ), jnp.float32)
        for step_index in range(STEPS):
            padded = pad_plane(adj_cur)
            source = vertical_source(columns_one, traces_one[:, step_index], seafloor_depth, 0, 0, NY, NZ)
            force_now = elastic_force(padded, lame_first, mu_eff, buoyancy)
            force_now = force_now.at[:, 2].add(buoyancy * source)
            fresh_now = 2.0 * adj_cur - adj_prev + step_squared * force_now
            forward_now = forward_one[:, step_index].astype(jnp.float32)
            kernel_lam, kernel_mu = accumulate(kernel_lam, kernel_mu, padded, pad_plane(forward_now), solid_mask)
            adj_prev = adj_cur
            adj_cur = fresh_now
        return adj_cur[0], kernel_lam, kernel_mu

    finals, lam_parts, mu_parts = lax.map(one_source, (adj_now, adj_later, forward_field, station_columns, station_traces))
    kernels = jnp.stack([jnp.sum(lam_parts, axis=0), jnp.sum(mu_parts, axis=0)]) * (1.0 / SOURCES)
    return finals, kernels
```

```python
import functools

import jax
import jax.numpy as jnp
from jax import lax
from jax.experimental import pallas as pl
from jax.experimental.pallas import tpu as pltpu
from jax.sharding import PartitionSpec as P

STEPS = 3
TIME_SCALE = 0.04
MESH = pl.DeviceIdType.MESH
LANES = 128
PITCH = 32
FIRST = 8
XPEERS = 4
PACKS = 13
DIRS = ((-1, 0), (1, 0), (0, -1), (0, 1), (-1, -1), (-1, 1), (1, -1), (1, 1))


def opposite(d):
    return DIRS.index((-DIRS[d][0], -DIRS[d][1]))


def kernel(
    adj_now, adj_later, forward, lame, shear, buoyancy, seafloor, columns, traces,
    adj_out, kernels_out,
    u, prev, fin, fraw, fw, fx_land, fy_send, fy_land,
    y_send, y_land, c_send, c_land,
    p_lame, p_shear, p_buoy, p_sea, p_cols, p_traces,
    c_lap, c_div, q_add, sea_cols, acc, pack, x_land, z_send, z_land, kout,
    load_sem, out_sem, halo_send, halo_recv, fwd_send, fwd_recv, x_sem_s, x_sem_r, z_sem_s, z_sem_r,
):
    tx, ty, src = lax.axis_index("tx"), lax.axis_index("ty"), lax.axis_index("src")
    ntx, nty = lax.axis_size("tx"), lax.axis_size("ty")
    half, xpos = src // XPEERS, lax.rem(src, XPEERS)

    def exists(d):
        dx, dy = DIRS[d]
        good = None
        for pos, step, count in ((tx, dx, ntx), (ty, dy, nty)):
            if step:
                here = (pos > 0) if step < 0 else (pos < count - 1)
                good = here if good is None else jnp.logical_and(good, here)
        return good

    def neighbour(d):
        dx, dy = DIRS[d]
        target = {}
        if dx:
            target["tx"] = tx + dx
        if dy:
            target["ty"] = ty + dy
        return target

    def src_peer(r):
        return {"src": half * XPEERS + lax.rem(xpos + r, XPEERS)}

    far = {"src": (1 - half) * XPEERS + xpos}

    loads = []
    for c in range(2):
        zs = pl.ds(c * LANES, LANES)
        for x in range(8):
            loads.append(
                (
                    adj_now.at[0, :, x, :, zs],
                    u.at[0, :, c, pl.ds((x + 1) * PITCH + FIRST, 16), :],
                    0,
                )
            )
    loads.append((forward.at[0], fraw, 1))
    loads.append((adj_later.at[0], prev, 2))
    loads.append((lame, p_lame, 3))
    loads.append((shear, p_shear, 4))
    loads.append((buoyancy, p_buoy, 5))
    loads.append((seafloor, p_sea, 6))
    loads.append((columns, p_cols, 7))
    loads.append((traces.at[0], p_traces, 8))
    copies = {}
    for n, (a, b, _) in enumerate(loads):
        copy = pltpu.make_async_copy(a, b, load_sem.at[n])
        copy.start()
        copies[n] = copy

    barrier = pltpu.get_barrier_semaphore()
    expected = jnp.int32(XPEERS)
    for d in range(8):
        there = exists(d)
        expected = expected + there.astype(jnp.int32)

        @pl.when(there)
        def _(d=d):
            pl.semaphore_signal(barrier, inc=1, device_id=neighbour(d), device_id_type=MESH)

    for r in range(1, XPEERS):
        pl.semaphore_signal(barrier, inc=1, device_id=src_peer(r), device_id_type=MESH)
    pl.semaphore_signal(barrier, inc=1, device_id=far, device_id_type=MESH)
    pl.semaphore_wait(barrier, expected)

    def x_rows(t, plane):
        return u.at[t, :, :, pl.ds(plane * PITCH + FIRST, 16), :]

    def halo_source(t, d):
        if d == 0:
            return x_rows(t, 1)
        if d == 1:
            return x_rows(t, 8)
        if d < 4:
            return y_send.at[t, d - 2]
        return c_send.at[t, d - 4]

    def halo_target(t, d):
        if d == 0:
            return x_rows(t, 0)
        if d == 1:
            return x_rows(t, 9)
        if d < 4:
            return y_land.at[t, d - 2]
        return c_land.at[t, d - 4]

    def halo_copy(t, d, arrive):
        side = d if arrive else opposite(d)
        return pltpu.make_async_remote_copy(
            src_ref=halo_source(t, d),
            dst_ref=halo_target(t, side),
            send_sem=halo_send.at[t, d],
            recv_sem=halo_recv.at[t, side],
            device_id=neighbour(d),
            device_id_type=MESH,
        )

    def corner_row(d):
        dx, dy = DIRS[d]
        return (1 if dx < 0 else 8) * PITCH + (FIRST if dy < 0 else FIRST + 15)

    def send_halo(t):
        for d in range(2):

            @pl.when(exists(d))
            def _(d=d):
                halo_copy(t, d, False).start()

        for k in range(3):
            for c in range(2):
                y_send[t, 0, k, c] = u[t, k, c, pl.ds(PITCH + FIRST, 8, stride=PITCH), :]
                y_send[t, 1, k, c] = u[t, k, c, pl.ds(PITCH + FIRST + 15, 8, stride=PITCH), :]
        for d in range(4, 8):
            for k in range(2):
                for c in range(2):
                    row = corner_row(d)
                    c_send[t, d - 4, pl.ds(2 * k + c, 1), :] = u[t, k, c, pl.ds(row, 1), :]
        for d in range(2, 8):

            @pl.when(exists(d))
            def _(d=d):
                halo_copy(t, d, False).start()

    def receive_halo(t):
        for d in range(8):

            @pl.when(exists(d))
            def _(d=d):
                halo_copy(t, d, True).wait_recv()

        for k in range(3):
            for c in range(2):
                u[t, k, c, pl.ds(PITCH + FIRST - 1, 8, stride=PITCH), :] = y_land[t, 0, k, c]
                u[t, k, c, pl.ds(PITCH + FIRST + 16, 8, stride=PITCH), :] = y_land[t, 1, k, c]
        for d in range(4, 8):
            dx, dy = DIRS[d]
            row = (0 if dx < 0 else 9) * PITCH + (FIRST - 1 if dy < 0 else FIRST + 16)
            for k in range(2):
                for c in range(2):
                    u[t, k, c, pl.ds(row, 1), :] = c_land[t, d - 4, pl.ds(2 * k + c, 1), :]

    def forward_copy(n, d, arrive):
        side = d if arrive else opposite(d)
        if n < STEPS:
            source = fraw.at[n, :, 0 if d == 0 else 7]
            target = fx_land.at[n, side]
        else:
            source, target = fy_send.at[d - 2], fy_land.at[side - 2]
        return pltpu.make_async_remote_copy(
            src_ref=source,
            dst_ref=target,
            send_sem=fwd_send.at[n, d],
            recv_sem=fwd_recv.at[n, side],
            device_id=neighbour(d),
            device_id_type=MESH,
        )

    def each_forward(n, act):
        for d in (0, 1) if n < STEPS else (2, 3):

            @pl.when(exists(d))
            def _(d=d):
                act(n, d)

    zero = jnp.zeros((16, LANES), jnp.float32)
    for d in range(2):

        @pl.when(jnp.logical_not(exists(d)))
        def _(d=d):
            plane = 0 if d == 0 else 9
            for t in range(STEPS):
                for k in range(3):
                    for c in range(2):
                        u[t, k, c, pl.ds(plane * PITCH + FIRST, 16), :] = zero
            fx_land[:, d] = jnp.zeros(fx_land.shape[:1] + fx_land.shape[2:], fx_land.dtype)

    for d in range(2, 4):

        @pl.when(jnp.logical_not(exists(d)))
        def _(d=d):
            for t in range(STEPS):
                y_land[t, d - 2] = jnp.zeros(y_land.shape[2:], jnp.float32)
            fy_land[d - 2] = jnp.zeros(fy_land.shape[1:], fy_land.dtype)

    for d in range(4, 8):

        @pl.when(jnp.logical_not(exists(d)))
        def _(d=d):
            for t in range(STEPS):
                c_land[t, d - 4] = jnp.zeros(c_land.shape[2:], jnp.float32)

    lane = lax.broadcasted_iota(jnp.int32, (16, LANES), 1)
    is_first, is_last = lane == 0, lane == LANES - 1

    def shift_z(pair):
        a, b = pair
        ua, ub = pltpu.roll(a, LANES - 1, 1), pltpu.roll(b, LANES - 1, 1)
        da, db = pltpu.roll(a, 1, 1), pltpu.roll(b, 1, 1)
        above = (jnp.where(is_last, ub, ua), jnp.where(is_last, 0.0, ub))
        below = (jnp.where(is_first, 0.0, da), jnp.where(is_first, da, db))
        return above, below

    def diff_z(pair):
        above, below = shift_z(pair)
        return [above[c] - below[c] for c in range(2)]

    for n in range(16):
        copies[n].wait()
    send_halo(0)
    copies[16].wait()
    each_forward(0, lambda n, d: forward_copy(n, d, False).start())

    def widen(n, carry):
        t, k = n // 3, lax.rem(n, 3)
        for x in range(8):
            rows = fraw[t, k, x].astype(jnp.float32)
            for c in range(2):
                fw[t, k, c, pl.ds((x + 1) * PITCH + FIRST, 16), :] = rows[:, c * LANES : (c + 1) * LANES]
        for c in range(2):
            for side in range(2):
                row = PITCH + FIRST + 15 * side
                fy_send[side, t, k, c] = fw[t, k, c, pl.ds(row, 8, stride=PITCH), :].astype(fy_send.dtype)
        return carry

    lax.fori_loop(0, 3 * STEPS, widen, 0)
    each_forward(STEPS, lambda n, d: forward_copy(n, d, False).start())

    for n in range(17, 24):
        copies[n].wait()
    sublane = lax.broadcasted_iota(jnp.int32, (16, 16), 0)
    sublane_lane = lax.broadcasted_iota(jnp.int32, (16, 16), 1)
    stations = p_cols.shape[1]
    y_of = lax.broadcasted_iota(jnp.int32, (16, stations), 0)
    total_y = 16 * nty

    def coefficients(x, carry):
        depth_row = jnp.broadcast_to(p_sea[pl.ds(x, 1), :].astype(jnp.float32), (16, 16))
        depth = jnp.sum(jnp.where(sublane == sublane_lane, depth_row, 0.0), axis=1, keepdims=True)
        depth = jnp.broadcast_to(depth, (16, LANES)).astype(jnp.int32)
        sea_cols[x] = depth
        column = (tx * 8 + x) * total_y + ty * 16 + y_of
        hit = jnp.broadcast_to(p_cols[...], (16, stations)) == column
        amps = []
        for t in range(STEPS):
            amp = jnp.broadcast_to(p_traces[pl.ds(t, 1), :], (16, stations))
            amp = jnp.sum(jnp.where(hit, amp, 0.0), axis=1, keepdims=True)
            amps.append(jnp.broadcast_to(amp, (16, LANES)))
        for c in range(2):
            zs = slice(c * LANES, (c + 1) * LANES)
            scaled = TIME_SCALE * p_buoy[x, :, zs]
            level = lane + c * LANES
            mu = jnp.where(level >= depth, p_shear[x, :, zs], 0.0)
            c_lap[c, x] = scaled * mu
            c_div[c, x] = scaled * (p_lame[x, :, zs] + mu)
            for t in range(STEPS):
                q_add[t, c, x] = jnp.where(level == depth, scaled * amps[t], 0.0)
        return carry

    lax.fori_loop(0, 8, coefficients, 0)

    def step(t):
        def row(x, carry):
            base = (x + 1) * PITCH + FIRST

            def at(k, c, dx, dy):
                return u[t, k, c, pl.ds(base + dx * PITCH + dy, 16), :]

            both = range(2)
            centre = [[at(k, c, 0, 0) for c in both] for k in range(3)]
            gx, gy, fresh = [], [], []
            lap, second = [], []
            for k in range(3):
                xp, xm = [at(k, c, 1, 0) for c in both], [at(k, c, -1, 0) for c in both]
                yp, ym = [at(k, c, 0, 1) for c in both], [at(k, c, 0, -1) for c in both]
                zp, zm = shift_z(centre[k])
                gx.append([xp[c] - xm[c] for c in both])
                gy.append([yp[c] - ym[c] for c in both])
                sums = [[a[c] + b[c] for c in both] for a, b in ((xp, xm), (yp, ym), (zp, zm))]
                lap.append([sums[0][c] + sums[1][c] + sums[2][c] - 6.0 * centre[k][c] for c in both])
                second.append([sums[k][c] - 2.0 * centre[k][c] for c in both])

            def cross(k):
                return [
                    (at(k, c, 1, 1) - at(k, c, -1, 1)) - (at(k, c, 1, -1) - at(k, c, -1, -1)) for c in both
                ]

            cross_0, cross_1 = cross(0), cross(1)
            dz_gx2, dz_gy2 = diff_z(gx[2]), diff_z(gy[2])
            dz_mix = diff_z([gx[0][c] + gy[1][c] for c in both])
            mixed = [
                [cross_1[c] + dz_gx2[c] for c in both],
                [cross_0[c] + dz_gy2[c] for c in both],
                dz_mix,
            ]
            for k in range(3):
                for c in both:
                    if t == 0:
                        old = prev[k, x, :, c * LANES : (c + 1) * LANES]
                    else:
                        old = u[t - 1, k, c, pl.ds(base, 16), :]
                    new = (
                        (2.0 * centre[k][c] - old)
                        + c_lap[c, x] * lap[k][c]
                        + c_div[c, x] * (second[k][c] + 0.25 * mixed[k][c])
                    )
                    if k == 2:
                        new = new + q_add[t, c, x]
                    if t < STEPS - 1:
                        u[t + 1, k, c, pl.ds(base, 16), :] = new
                    else:
                        fin[k, x, :, c * LANES : (c + 1) * LANES] = new
            return carry

        lax.fori_loop(0, 8, row, 0)

    def receive_forward(t):
        each_forward(t, lambda n, d: forward_copy(n, d, True).wait_recv())
        if t == 0:
            each_forward(STEPS, lambda n, d: forward_copy(n, d, True).wait_recv())
        for k in range(3):
            for side in range(2):
                plane = 9 * side
                rows = fx_land[t, side, k].astype(jnp.float32)
                for c in range(2):
                    fw[t, k, c, pl.ds(plane * PITCH + FIRST, 16), :] = rows[:, c * LANES : (c + 1) * LANES]
                    row = PITCH + (FIRST - 1 if side == 0 else FIRST + 16)
                    fw[t, k, c, pl.ds(row, 8, stride=PITCH), :] = fy_land[side, t, k, c].astype(jnp.float32)

    def accumulate(t):
        def row(x, carry):
            base = (x + 1) * PITCH + FIRST
            both = range(2)

            def gradient(ref, k):
                at = lambda c, dx, dy: ref[t, k, c, pl.ds(base + dx * PITCH + dy, 16), :]
                g_x = [at(c, 1, 0) - at(c, -1, 0) for c in both]
                g_y = [at(c, 0, 1) - at(c, 0, -1) for c in both]
                g_z = diff_z([at(c, 0, 0) for c in both])
                return g_x, g_y, g_z

            mu = div_u = div_f = None
            for k in range(3):
                gu, gf = gradient(u, k), gradient(fw, k)
                for d in range(3):
                    term = [gu[d][c] * gf[d][c] for c in both]
                    mu = term if mu is None else [mu[c] + term[c] for c in both]
                div_u = gu[k] if div_u is None else [div_u[c] + gu[k][c] for c in both]
                div_f = gf[k] if div_f is None else [div_f[c] + gf[k][c] for c in both]
            for c in both:
                lam = div_u[c] * div_f[c]
                if t == 0:
                    acc[0, c, x], acc[1, c, x] = lam, mu[c]
                else:
                    acc[0, c, x] = acc[0, c, x] + lam
                    acc[1, c, x] = acc[1, c, x] + mu[c]
            return carry

        lax.fori_loop(0, 8, row, 0)

    receive_halo(0)
    for t in range(STEPS - 1):
        step(t)
        send_halo(t + 1)
        each_forward(t + 1, lambda n, d: forward_copy(n, d, False).start())
        receive_forward(t)
        accumulate(t)
        receive_halo(t + 1)
    receive_forward(STEPS - 1)
    accumulate(STEPS - 1)

    lane8 = lax.broadcasted_iota(jnp.int32, (8, LANES), 1)
    even = lax.rem(lane8 // 32, 2) == 0
    low = lane8 < 64

    def quarters(v):
        w = []
        for a, b in ((v[0], v[1]), (v[2], v[3])):
            w.append(
                (
                    jnp.where(even, a, pltpu.roll(b, 32, 1)),
                    jnp.where(even, pltpu.roll(a, 96, 1), b),
                )
            )
        out = [None] * 4
        for odd in range(2):
            a, b = w[0][odd], w[1][odd]
            out[odd] = jnp.where(low, a, pltpu.roll(b, 64, 1))
            out[2 + odd] = jnp.where(low, pltpu.roll(a, 64, 1), b)
        return out

    def masked_mu(c, x, ys):
        return jnp.where(lane8 + c * LANES >= sea_cols[x, ys], acc[1, c, x, ys], 0.0)

    for s in range(2):
        ys = pl.ds(8 * s, 8)
        for g in range(2):
            n = 2 * s + g
            for first, tiles in (
                (0, [acc[0, 0, 4 * g + a, ys] for a in range(4)]),
                (5, [acc[0, 1, 4 * g + a, ys] for a in range(4)]),
                (9, [masked_mu(1, 4 * g + a, ys) for a in range(4)]),
            ):
                for q, tile in enumerate(quarters(tiles)):
                    pack[q, first + n] = tile
    rest = None
    for x in range(8):
        for s in range(2):
            tile = masked_mu(0, x, pl.ds(8 * s, 8))
            tile = pltpu.roll(tile, (2 * (2 * x + s) + 2) % LANES, 1)
            rest = tile if rest is None else rest + tile
    for q in range(XPEERS):
        pack[q, 4] = rest

    def x_copy(r):
        return pltpu.make_async_remote_copy(
            src_ref=pack.at[lax.rem(xpos + r, XPEERS)],
            dst_ref=x_land.at[r - 1],
            send_sem=x_sem_s.at[r - 1],
            recv_sem=x_sem_r.at[r - 1],
            device_id=src_peer(r),
            device_id_type=MESH,
        )

    for r in (2, 1, 3):
        x_copy(r).start()

    step(STEPS - 1)
    final_copy = pltpu.make_async_copy(fin, adj_out.at[0], out_sem.at[0])
    final_copy.start()

    for r in (1, 3, 2):
        x_copy(r).wait_recv()

    def total(n):
        return pack[xpos, n] + x_land[0, n] + x_land[1, n] + x_land[2, n]

    def z_copy(first, count):
        return pltpu.make_async_remote_copy(
            src_ref=z_send.at[pl.ds(first, count)],
            dst_ref=z_land.at[pl.ds(first, count)],
            send_sem=z_sem_s,
            recv_sem=z_sem_r,
            device_id=far,
            device_id_type=MESH,
        )

    for n in range(PACKS):
        z_send[n] = total(n)

    @pl.when(half == 0)
    def _():
        z_copy(5, 8).start()

    @pl.when(half == 1)
    def _():
        z_copy(0, 5).start()

    scale = 0.25 / lax.axis_size("src")

    def unpack(kind, n, tile):
        s, g = n // 2, n % 2
        for a in range(4):
            part = pltpu.roll(tile, (LANES - 32 * a) % LANES, 1) if a else tile
            kout[kind, 4 * g + a, pl.ds(8 * s, 8), :] = part[:, :32]

    @pl.when(half == 0)
    def _():
        z_copy(0, 5).wait_recv()
        for n in range(4):
            unpack(0, n, (z_send[n] + z_land[n]) * scale)
        rest = jnp.where(xpos == XPEERS - 1, (z_send[4] + z_land[4]) * scale, 0.0)
        tail = jnp.logical_and(lane8 >= 30, lane8 < 32)
        for x in range(8):
            for s in range(2):
                tile = pltpu.roll(rest, (30 - 2 * (2 * x + s)) % LANES, 1)
                kout[1, x, pl.ds(8 * s, 8), :] = jnp.where(tail, tile, 0.0)[:, :32]

    @pl.when(half == 1)
    def _():
        z_copy(5, 8).wait_recv()
        for kind in range(2):
            for n in range(4):
                m = 5 + 4 * kind + n
                unpack(kind, n, (z_send[m] + z_land[m]) * scale)

    kernels_copy = pltpu.make_async_copy(kout, kernels_out, out_sem.at[1])
    kernels_copy.start()

    for t in range(STEPS):
        for d in range(8):

            @pl.when(exists(d))
            def _(t=t, d=d):
                halo_copy(t, d, False).wait_send()

    for n in range(STEPS + 1):
        each_forward(n, lambda n, d: forward_copy(n, d, False).wait_send())
    for r in range(1, XPEERS):
        x_copy(r).wait_send()

    @pl.when(half == 0)
    def _():
        z_copy(5, 8).wait_send()

    @pl.when(half == 1)
    def _():
        z_copy(0, 5).wait_send()

    final_copy.wait()
    kernels_copy.wait()


def body(adj_now, adj_later, forward_field, lame_first, shear, buoyancy, seafloor_depth, station_columns, station_traces):
    f32, bf16 = jnp.float32, jnp.bfloat16
    vmem, dma = pltpu.VMEM, pltpu.SemaphoreType.DMA
    stations = station_columns.shape[1]
    anywhere = pl.BlockSpec(memory_space=pl.ANY)
    rows = 10 * PITCH
    return pl.pallas_call(
        kernel,
        name="adjoint",
        out_shape=(
            jax.ShapeDtypeStruct((1, 3, 8, 16, 256), f32),
            jax.ShapeDtypeStruct((2, 8, 16, 32), f32),
        ),
        in_specs=[anywhere] * 9,
        out_specs=(anywhere, anywhere),
        scratch_shapes=[
            vmem((STEPS, 3, 2, rows, LANES), f32),
            vmem((3, 8, 16, 256), f32),
            vmem((3, 8, 16, 256), f32),
            vmem((STEPS, 3, 8, 16, 256), bf16),
            vmem((STEPS, 3, 2, rows, LANES), f32),
            vmem((STEPS, 2, 3, 16, 256), bf16),
            vmem((2, STEPS, 3, 2, 8, LANES), bf16),
            vmem((2, STEPS, 3, 2, 8, LANES), bf16),
            vmem((STEPS, 2, 3, 2, 8, LANES), f32),
            vmem((STEPS, 2, 3, 2, 8, LANES), f32),
            vmem((STEPS, 4, 4, LANES), f32),
            vmem((STEPS, 4, 4, LANES), f32),
            vmem((8, 16, 256), f32),
            vmem((8, 16, 256), f32),
            vmem((8, 16, 256), f32),
            vmem((8, 16), jnp.int32),
            vmem((1, stations), jnp.int32),
            vmem((STEPS, stations), f32),
            vmem((2, 8, 16, LANES), f32),
            vmem((2, 8, 16, LANES), f32),
            vmem((STEPS, 2, 8, 16, LANES), f32),
            vmem((8, 16, LANES), jnp.int32),
            vmem((2, 2, 8, 16, LANES), f32),
            vmem((XPEERS, PACKS, 8, LANES), f32),
            vmem((3, PACKS, 8, LANES), f32),
            vmem((PACKS, 8, LANES), f32),
            vmem((PACKS, 8, LANES), f32),
            vmem((2, 8, 16, 32), f32),
            dma((24,)),
            dma((2,)),
            dma((STEPS, 8)),
            dma((STEPS, 8)),
            dma((STEPS + 1, 4)),
            dma((STEPS + 1, 4)),
            dma((3,)),
            dma((3,)),
            dma,
            dma,
        ],
        compiler_params=pltpu.CompilerParams(
            collective_id=0, has_side_effects=True, vmem_limit_bytes=24 << 20
        ),
    )(
        adj_now, adj_later, forward_field, lame_first, shear, buoyancy, seafloor_depth,
        station_columns, station_traces,
    )


def solution(mesh):
    in_specs = (
        P("src", None, "tx", "ty", None),
        P("src", None, "tx", "ty", None),
        P("src", None, None, "tx", "ty", None),
        P("tx", "ty", None),
        P("tx", "ty", None),
        P("tx", "ty", None),
        P("tx", "ty"),
        P("src", None),
        P("src", None, None),
    )
    out_specs = (P("src", None, "tx", "ty", None), P(None, "tx", "ty", "src"))
    return jax.shard_map(body, mesh=mesh, in_specs=in_specs, out_specs=out_specs, check_vma=False)
```

```python
import functools

import jax
import jax.numpy as jnp
from jax import lax
from jax.experimental import pallas as pl
from jax.experimental.pallas import tpu as pltpu
from jax.sharding import PartitionSpec as P

STEPS = 3
TIME_SCALE = 0.04
MESH = pl.DeviceIdType.MESH
LANES = 128
PITCH = 32
FIRST = 8
XPEERS = 4
PACKS = 13
DIRS = ((-1, 0), (1, 0), (0, -1), (0, 1), (-1, -1), (-1, 1), (1, -1), (1, 1))


def opposite(d):
    return DIRS.index((-DIRS[d][0], -DIRS[d][1]))


def kernel(
    adj_now, adj_later, forward, lame, shear, buoyancy, seafloor, columns, traces,
    adj_out, kernels_out,
    u, prev, fin, fraw, fw, fx_land, fy_send, fy_land,
    y_send, y_land, c_send, c_land,
    p_lame, p_shear, p_buoy, p_sea, p_cols, p_traces,
    c_lap, c_div, q_add, sea_cols, acc, pack, x_land, z_send, z_land, kout,
    load_sem, out_sem, halo_send, halo_recv, fwd_send, fwd_recv, x_sem_s, x_sem_r, z_sem_s, z_sem_r, far_ready,
):
    tx, ty, src = lax.axis_index("tx"), lax.axis_index("ty"), lax.axis_index("src")
    ntx, nty = lax.axis_size("tx"), lax.axis_size("ty")
    half, xpos = src // XPEERS, lax.rem(src, XPEERS)

    def exists(d):
        dx, dy = DIRS[d]
        good = None
        for pos, step, count in ((tx, dx, ntx), (ty, dy, nty)):
            if step:
                here = (pos > 0) if step < 0 else (pos < count - 1)
                good = here if good is None else jnp.logical_and(good, here)
        return good

    def neighbour(d):
        dx, dy = DIRS[d]
        target = {}
        if dx:
            target["tx"] = tx + dx
        if dy:
            target["ty"] = ty + dy
        return target

    def src_peer(r):
        return {"src": half * XPEERS + lax.rem(xpos + r, XPEERS)}

    far = {"src": (1 - half) * XPEERS + xpos}

    loads = []
    for c in range(2):
        zs = pl.ds(c * LANES, LANES)
        for x in range(8):
            loads.append(
                (
                    adj_now.at[0, :, x, :, zs],
                    u.at[0, :, c, pl.ds((x + 1) * PITCH + FIRST, 16), :],
                    0,
                )
            )
    loads.append((forward.at[0], fraw, 1))
    loads.append((adj_later.at[0], prev, 2))
    loads.append((lame, p_lame, 3))
    loads.append((shear, p_shear, 4))
    loads.append((buoyancy, p_buoy, 5))
    loads.append((seafloor, p_sea, 6))
    loads.append((columns, p_cols, 7))
    loads.append((traces, p_traces, 8))
    copies = {}
    for n, (a, b, _) in enumerate(loads):
        copy = pltpu.make_async_copy(a, b, load_sem.at[n])
        copy.start()
        copies[n] = copy

    barrier = pltpu.get_barrier_semaphore()
    expected = XPEERS - 1 + half
    for d in range(8):
        there = exists(d)
        expected = expected + there.astype(jnp.int32)

        @pl.when(there)
        def _(d=d):
            pl.semaphore_signal(barrier, inc=1, device_id=neighbour(d), device_id_type=MESH)

    for r in range(1, XPEERS):
        pl.semaphore_signal(barrier, inc=1, device_id=src_peer(r), device_id_type=MESH)

    @pl.when(half == 0)
    def _():
        pl.semaphore_signal(barrier, inc=1, device_id=far, device_id_type=MESH)

    pl.semaphore_wait(barrier, expected)

    @pl.when(half == 1)
    def _():
        pl.semaphore_signal(far_ready, inc=1, device_id=far, device_id_type=MESH)


    def x_rows(t, plane):
        return u.at[t, :, :, pl.ds(plane * PITCH + FIRST, 16), :]

    def halo_source(t, d):
        if d == 0:
            return x_rows(t, 1)
        if d == 1:
            return x_rows(t, 8)
        if d < 4:
            return y_send.at[t, d - 2]
        return c_send.at[t, d - 4]

    def halo_target(t, d):
        if d == 0:
            return x_rows(t, 0)
        if d == 1:
            return x_rows(t, 9)
        if d < 4:
            return y_land.at[t, d - 2]
        return c_land.at[t, d - 4]

    def halo_copy(t, d, arrive):
        side = d if arrive else opposite(d)
        return pltpu.make_async_remote_copy(
            src_ref=halo_source(t, d),
            dst_ref=halo_target(t, side),
            send_sem=halo_send.at[t, d],
            recv_sem=halo_recv.at[t, side],
            device_id=neighbour(d),
            device_id_type=MESH,
        )

    def corner_row(d):
        dx, dy = DIRS[d]
        return (1 if dx < 0 else 8) * PITCH + (FIRST if dy < 0 else FIRST + 15)

    def start(t, directions):
        for d in directions:

            @pl.when(exists(d))
            def _(d=d):
                halo_copy(t, d, False).start()

    def send_corners(t):
        for d in range(4, 8):
            for k in range(2):
                for c in range(2):
                    row = corner_row(d)
                    c_send[t, d - 4, pl.ds(2 * k + c, 1), :] = u[t, k, c, pl.ds(row, 1), :]
        start(t, range(4, 8))

    def send_y(t):
        for k in range(3):
            for c in range(2):
                y_send[t, 0, k, c] = u[t, k, c, pl.ds(PITCH + FIRST, 8, stride=PITCH), :]
                y_send[t, 1, k, c] = u[t, k, c, pl.ds(PITCH + FIRST + 15, 8, stride=PITCH), :]
        start(t, range(2, 4))

    def receive_halo(t):
        for d in range(8):

            @pl.when(exists(d))
            def _(d=d):
                halo_copy(t, d, True).wait_recv()

        for k in range(3):
            for c in range(2):
                u[t, k, c, pl.ds(PITCH + FIRST - 1, 8, stride=PITCH), :] = y_land[t, 0, k, c]
                u[t, k, c, pl.ds(PITCH + FIRST + 16, 8, stride=PITCH), :] = y_land[t, 1, k, c]
        for d in range(4, 8):
            dx, dy = DIRS[d]
            row = (0 if dx < 0 else 9) * PITCH + (FIRST - 1 if dy < 0 else FIRST + 16)
            for k in range(2):
                for c in range(2):
                    u[t, k, c, pl.ds(row, 1), :] = c_land[t, d - 4, pl.ds(2 * k + c, 1), :]

    for d in range(2):

        @pl.when(exists(d))
        def _(d=d):
            side = opposite(d)
            for c in range(2):
                pltpu.make_async_remote_copy(
                    src_ref=adj_now.at[0, :, 7 * d, :, pl.ds(c * LANES, LANES)],
                    dst_ref=u.at[0, :, c, pl.ds((9 if side else 0) * PITCH + FIRST, 16), :],
                    send_sem=halo_send.at[0, d],
                    recv_sem=halo_recv.at[0, side],
                    device_id=neighbour(d),
                    device_id_type=MESH,
                ).start()

    def forward_copy(n, d, arrive):
        side = d if arrive else opposite(d)
        if n < STEPS:
            source = fraw.at[n, :, 0 if d == 0 else 7]
            target = fx_land.at[n, side]
        else:
            source, target = fy_send.at[d - 2], fy_land.at[side - 2]
        return pltpu.make_async_remote_copy(
            src_ref=source,
            dst_ref=target,
            send_sem=fwd_send.at[n, d],
            recv_sem=fwd_recv.at[n, side],
            device_id=neighbour(d),
            device_id_type=MESH,
        )

    def each_forward(n, act):
        for d in (0, 1) if n < STEPS else (2, 3):

            @pl.when(exists(d))
            def _(d=d):
                act(n, d)

    lane = lax.broadcasted_iota(jnp.int32, (16, LANES), 1)
    is_first, is_last = lane == 0, lane == LANES - 1

    def shift_z(pair):
        a, b = pair
        ua, ub = pltpu.roll(a, LANES - 1, 1), pltpu.roll(b, LANES - 1, 1)
        da, db = pltpu.roll(a, 1, 1), pltpu.roll(b, 1, 1)
        above = (jnp.where(is_last, ub, ua), jnp.where(is_last, 0.0, ub))
        below = (jnp.where(is_first, 0.0, da), jnp.where(is_first, da, db))
        return above, below

    def diff_z(pair):
        above, below = shift_z(pair)
        return [above[c] - below[c] for c in range(2)]

    for n in range(16):
        copies[n].wait()
    send_corners(0)
    send_y(0)
    copies[16].wait()
    each_forward(0, lambda n, d: forward_copy(n, d, False).start())

    zero = jnp.zeros((16, LANES), jnp.float32)
    for d in range(2):

        @pl.when(jnp.logical_not(exists(d)))
        def _(d=d):
            plane = 0 if d == 0 else 9
            for t in range(STEPS):
                for k in range(3):
                    for c in range(2):
                        u[t, k, c, pl.ds(plane * PITCH + FIRST, 16), :] = zero
            fx_land[:, d] = jnp.zeros(fx_land.shape[:1] + fx_land.shape[2:], fx_land.dtype)

    for d in range(2, 4):

        @pl.when(jnp.logical_not(exists(d)))
        def _(d=d):
            for t in range(STEPS):
                y_land[t, d - 2] = jnp.zeros(y_land.shape[2:], jnp.float32)
            fy_land[d - 2] = jnp.zeros(fy_land.shape[1:], fy_land.dtype)

    for d in range(4, 8):

        @pl.when(jnp.logical_not(exists(d)))
        def _(d=d):
            for t in range(STEPS):
                c_land[t, d - 4] = jnp.zeros(c_land.shape[2:], jnp.float32)


    def widen(n, carry):
        t, k = n // 3, lax.rem(n, 3)
        for x in range(8):
            rows = fraw[t, k, x].astype(jnp.float32)
            for c in range(2):
                fw[t, k, c, pl.ds((x + 1) * PITCH + FIRST, 16), :] = rows[:, c * LANES : (c + 1) * LANES]
        for c in range(2):
            for side in range(2):
                row = PITCH + FIRST + 15 * side
                fy_send[side, t, k, c] = fw[t, k, c, pl.ds(row, 8, stride=PITCH), :].astype(fy_send.dtype)
        return carry

    lax.fori_loop(0, 3 * STEPS, widen, 0)
    each_forward(STEPS, lambda n, d: forward_copy(n, d, False).start())

    for n in range(17, 24):
        copies[n].wait()
    sublane = lax.broadcasted_iota(jnp.int32, (16, 16), 0)
    sublane_lane = lax.broadcasted_iota(jnp.int32, (16, 16), 1)
    stations = p_cols.shape[1]
    y_of = lax.broadcasted_iota(jnp.int32, (16, stations), 0)
    total_y = 16 * nty

    def coefficients(x, carry):
        depth_row = jnp.broadcast_to(p_sea[pl.ds(x, 1), :].astype(jnp.float32), (16, 16))
        depth = jnp.sum(jnp.where(sublane == sublane_lane, depth_row, 0.0), axis=1, keepdims=True)
        depth = jnp.broadcast_to(depth, (16, LANES)).astype(jnp.int32)
        sea_cols[x] = depth
        column = (tx * 8 + x) * total_y + ty * 16 + y_of
        hit = jnp.broadcast_to(p_cols[...], (16, stations)) == column
        amps = []
        for t in range(STEPS):
            amp = jnp.broadcast_to(p_traces[t], (16, stations))
            amp = jnp.sum(jnp.where(hit, amp, 0.0), axis=1, keepdims=True)
            amps.append(jnp.broadcast_to(amp, (16, LANES)))
        for c in range(2):
            zs = slice(c * LANES, (c + 1) * LANES)
            scaled = TIME_SCALE * p_buoy[x, :, zs]
            level = lane + c * LANES
            mu = jnp.where(level >= depth, p_shear[x, :, zs], 0.0)
            c_lap[c, x] = scaled * mu
            c_div[c, x] = scaled * (p_lame[x, :, zs] + mu)
            for t in range(STEPS):
                q_add[t, c, x] = jnp.where(level == depth, scaled * amps[t], 0.0)
        return carry

    lax.fori_loop(0, 8, coefficients, 0)

    def step(t, first, count, stride):
        def row(i, carry):
            x = first + i * stride
            base = (x + 1) * PITCH + FIRST

            def at(k, c, dx, dy):
                return u[t, k, c, pl.ds(base + dx * PITCH + dy, 16), :]

            both = range(2)
            centre = [[at(k, c, 0, 0) for c in both] for k in range(3)]
            gx, gy, fresh = [], [], []
            lap, second = [], []
            for k in range(3):
                xp, xm = [at(k, c, 1, 0) for c in both], [at(k, c, -1, 0) for c in both]
                yp, ym = [at(k, c, 0, 1) for c in both], [at(k, c, 0, -1) for c in both]
                zp, zm = shift_z(centre[k])
                gx.append([xp[c] - xm[c] for c in both])
                gy.append([yp[c] - ym[c] for c in both])
                sums = [[a[c] + b[c] for c in both] for a, b in ((xp, xm), (yp, ym), (zp, zm))]
                lap.append([sums[0][c] + sums[1][c] + sums[2][c] - 6.0 * centre[k][c] for c in both])
                second.append([sums[k][c] - 2.0 * centre[k][c] for c in both])

            def cross(k):
                return [
                    (at(k, c, 1, 1) - at(k, c, -1, 1)) - (at(k, c, 1, -1) - at(k, c, -1, -1)) for c in both
                ]

            cross_0, cross_1 = cross(0), cross(1)
            dz_gx2, dz_gy2 = diff_z(gx[2]), diff_z(gy[2])
            dz_mix = diff_z([gx[0][c] + gy[1][c] for c in both])
            mixed = [
                [cross_1[c] + dz_gx2[c] for c in both],
                [cross_0[c] + dz_gy2[c] for c in both],
                dz_mix,
            ]
            for k in range(3):
                for c in both:
                    if t == 0:
                        old = prev[k, x, :, c * LANES : (c + 1) * LANES]
                    else:
                        old = u[t - 1, k, c, pl.ds(base, 16), :]
                    new = (
                        (2.0 * centre[k][c] - old)
                        + c_lap[c, x] * lap[k][c]
                        + c_div[c, x] * (second[k][c] + 0.25 * mixed[k][c])
                    )
                    if k == 2:
                        new = new + q_add[t, c, x]
                    if t < STEPS - 1:
                        u[t + 1, k, c, pl.ds(base, 16), :] = new
                    else:
                        fin[k, x, :, c * LANES : (c + 1) * LANES] = new
            return carry

        lax.fori_loop(0, count, row, 0)

    def receive_forward(t):
        each_forward(t, lambda n, d: forward_copy(n, d, True).wait_recv())
        if t == 0:
            each_forward(STEPS, lambda n, d: forward_copy(n, d, True).wait_recv())
        for k in range(3):
            for side in range(2):
                plane = 9 * side
                rows = fx_land[t, side, k].astype(jnp.float32)
                for c in range(2):
                    fw[t, k, c, pl.ds(plane * PITCH + FIRST, 16), :] = rows[:, c * LANES : (c + 1) * LANES]
                    row = PITCH + (FIRST - 1 if side == 0 else FIRST + 16)
                    fw[t, k, c, pl.ds(row, 8, stride=PITCH), :] = fy_land[side, t, k, c].astype(jnp.float32)

    def diff_z_half(a, b, c):
        if c == 0:
            above = jnp.where(is_last, pltpu.roll(b, LANES - 1, 1), pltpu.roll(a, LANES - 1, 1))
            below = jnp.where(is_first, 0.0, pltpu.roll(a, 1, 1))
        else:
            above = jnp.where(is_last, 0.0, pltpu.roll(b, LANES - 1, 1))
            below = jnp.where(is_first, pltpu.roll(a, 1, 1), pltpu.roll(b, 1, 1))
        return above - below

    def accumulate(t, both=(0, 1)):
        def row(x, carry):
            base = (x + 1) * PITCH + FIRST

            def gradient(ref, k):
                at = lambda c, dx, dy: ref[t, k, c, pl.ds(base + dx * PITCH + dy, 16), :]
                g_x = {c: at(c, 1, 0) - at(c, -1, 0) for c in both}
                g_y = {c: at(c, 0, 1) - at(c, 0, -1) for c in both}
                pair = [at(c, 0, 0) for c in range(2)]
                if len(both) == 2:
                    g_z = diff_z(pair)
                else:
                    g_z = {both[0]: diff_z_half(*pair, both[0])}
                return g_x, g_y, g_z

            mu = div_u = div_f = None
            for k in range(3):
                gu, gf = gradient(u, k), gradient(fw, k)
                for d in range(3):
                    term = {c: gu[d][c] * gf[d][c] for c in both}
                    mu = term if mu is None else {c: mu[c] + term[c] for c in both}
                div_u = gu[k] if div_u is None else {c: div_u[c] + gu[k][c] for c in both}
                div_f = gf[k] if div_f is None else {c: div_f[c] + gf[k][c] for c in both}
            for c in both:
                lam = div_u[c] * div_f[c]
                if t == 0:
                    acc[0, c, x], acc[1, c, x] = lam, mu[c]
                else:
                    acc[0, c, x] = acc[0, c, x] + lam
                    acc[1, c, x] = acc[1, c, x] + mu[c]
            return carry

        lax.fori_loop(0, 8, row, 0)

    receive_halo(0)
    for t in range(STEPS - 1):
        step(t, 0, 2, 7)
        start(t + 1, range(2))
        send_corners(t + 1)
        step(t, 1, 6, 1)
        send_y(t + 1)
        each_forward(t + 1, lambda n, d: forward_copy(n, d, False).start())
        receive_forward(t)
        accumulate(t)
        receive_halo(t + 1)
    lane8 = lax.broadcasted_iota(jnp.int32, (8, LANES), 1)
    even = lax.rem(lane8 // 32, 2) == 0
    low = lane8 < 64

    def quarters(v):
        w = []
        for a, b in ((v[0], v[1]), (v[2], v[3])):
            w.append(
                (
                    jnp.where(even, a, pltpu.roll(b, 32, 1)),
                    jnp.where(even, pltpu.roll(a, 96, 1), b),
                )
            )
        out = [None] * 4
        for odd in range(2):
            a, b = w[0][odd], w[1][odd]
            out[odd] = jnp.where(low, a, pltpu.roll(b, 64, 1))
            out[2 + odd] = jnp.where(low, pltpu.roll(a, 64, 1), b)
        return out

    def masked_mu(c, x, ys):
        return jnp.where(lane8 + c * LANES >= sea_cols[x, ys], acc[1, c, x, ys], 0.0)

    parts = ((0, 5), (5, 8))

    def fill(c):
        for s in range(2):
            ys = pl.ds(8 * s, 8)
            for g in range(2):
                n = parts[c][0] + 2 * s + g
                for q, tile in enumerate(quarters([acc[0, c, 4 * g + a, ys] for a in range(4)])):
                    pack[q, n] = tile
                if c == 1:
                    for q, tile in enumerate(quarters([masked_mu(1, 4 * g + a, ys) for a in range(4)])):
                        pack[q, n + 4] = tile
        if c == 0:
            rest = None
            for x in range(8):
                for s in range(2):
                    tile = masked_mu(0, x, pl.ds(8 * s, 8))
                    tile = pltpu.roll(tile, (2 * (2 * x + s) + 2) % LANES, 1)
                    rest = tile if rest is None else rest + tile
            for q in range(XPEERS):
                pack[q, 4] = rest

    def x_copy(r, c):
        rows = pl.ds(*parts[c])
        return pltpu.make_async_remote_copy(
            src_ref=pack.at[lax.rem(xpos + r, XPEERS), rows],
            dst_ref=x_land.at[r - 1, rows],
            send_sem=x_sem_s.at[r - 1, c],
            recv_sem=x_sem_r.at[r - 1, c],
            device_id=src_peer(r),
            device_id_type=MESH,
        )

    def x_total(c):
        for r in (1, 3, 2):
            x_copy(r, c).wait_recv()
        for n in range(parts[c][0], sum(parts[c])):
            z_send[n] = pack[xpos, n] + x_land[0, n] + x_land[1, n] + x_land[2, n]

    def z_copy(c):
        rows = pl.ds(*parts[c])
        return pltpu.make_async_remote_copy(
            src_ref=z_send.at[rows],
            dst_ref=z_land.at[rows],
            send_sem=z_sem_s,
            recv_sem=z_sem_r,
            device_id=far,
            device_id_type=MESH,
        )

    receive_forward(STEPS - 1)
    for mine in range(2):

        @pl.when(half == mine)
        def _(mine=mine):
            for c in (1 - mine, mine):
                accumulate(STEPS - 1, (c,))
                fill(c)
                for r in (2, 1, 3):
                    x_copy(r, c).start()
            x_total(1 - mine)
            if mine == 0:
                pl.semaphore_wait(far_ready, 1)
            z_copy(1 - mine).start()

    step(STEPS - 1, 0, 8, 1)
    final_copy = pltpu.make_async_copy(fin, adj_out.at[0], out_sem.at[0])
    final_copy.start()

    scale = 0.25 / lax.axis_size("src")

    def unpack(kind, n, tile):
        s, g = n // 2, n % 2
        for a in range(4):
            part = pltpu.roll(tile, (LANES - 32 * a) % LANES, 1) if a else tile
            kout[kind, 4 * g + a, pl.ds(8 * s, 8), :] = part[:, :32]

    @pl.when(half == 0)
    def _():
        x_total(0)
        z_copy(0).wait_recv()
        for n in range(4):
            unpack(0, n, (z_send[n] + z_land[n]) * scale)
        rest = jnp.where(xpos == XPEERS - 1, (z_send[4] + z_land[4]) * scale, 0.0)
        tail = jnp.logical_and(lane8 >= 30, lane8 < 32)
        for x in range(8):
            for s in range(2):
                tile = pltpu.roll(rest, (30 - 2 * (2 * x + s)) % LANES, 1)
                kout[1, x, pl.ds(8 * s, 8), :] = jnp.where(tail, tile, 0.0)[:, :32]

    @pl.when(half == 1)
    def _():
        x_total(1)
        z_copy(1).wait_recv()
        for kind in range(2):
            for n in range(4):
                m = 5 + 4 * kind + n
                unpack(kind, n, (z_send[m] + z_land[m]) * scale)

    kernels_copy = pltpu.make_async_copy(kout, kernels_out, out_sem.at[1])
    kernels_copy.start()

    for t in range(STEPS):
        for d in range(8):

            @pl.when(exists(d))
            def _(t=t, d=d):
                halo_copy(t, d, False).wait_send()

    for n in range(STEPS + 1):
        each_forward(n, lambda n, d: forward_copy(n, d, False).wait_send())
    for r in range(1, XPEERS):
        for c in range(2):
            x_copy(r, c).wait_send()

    @pl.when(half == 0)
    def _():
        z_copy(1).wait_send()

    @pl.when(half == 1)
    def _():
        z_copy(0).wait_send()

    final_copy.wait()
    kernels_copy.wait()


def body(adj_now, adj_later, forward_field, lame_first, shear, buoyancy, seafloor_depth, station_columns, station_traces):
    f32, bf16 = jnp.float32, jnp.bfloat16
    vmem, dma = pltpu.VMEM, pltpu.SemaphoreType.DMA
    stations = station_columns.shape[1]
    anywhere = pl.BlockSpec(memory_space=pltpu.HBM)
    rows = 10 * PITCH
    return pl.pallas_call(
        kernel,
        name="adjoint",
        out_shape=(
            jax.ShapeDtypeStruct((1, 3, 8, 16, 256), f32),
            jax.ShapeDtypeStruct((2, 8, 16, 32), f32),
        ),
        in_specs=[anywhere] * 9,
        out_specs=(anywhere, anywhere),
        scratch_shapes=[
            vmem((STEPS, 3, 2, rows, LANES), f32),
            vmem((3, 8, 16, 256), f32),
            vmem((3, 8, 16, 256), f32),
            vmem((STEPS, 3, 8, 16, 256), bf16),
            vmem((STEPS, 3, 2, rows, LANES), f32),
            vmem((STEPS, 2, 3, 16, 256), bf16),
            vmem((2, STEPS, 3, 2, 8, LANES), bf16),
            vmem((2, STEPS, 3, 2, 8, LANES), bf16),
            vmem((STEPS, 2, 3, 2, 8, LANES), f32),
            vmem((STEPS, 2, 3, 2, 8, LANES), f32),
            vmem((STEPS, 4, 4, LANES), f32),
            vmem((STEPS, 4, 4, LANES), f32),
            vmem((8, 16, 256), f32),
            vmem((8, 16, 256), f32),
            vmem((8, 16, 256), f32),
            vmem((8, 16), jnp.int32),
            vmem((1, stations), jnp.int32),
            vmem((STEPS, 1, stations), f32),
            vmem((2, 8, 16, LANES), f32),
            vmem((2, 8, 16, LANES), f32),
            vmem((STEPS, 2, 8, 16, LANES), f32),
            vmem((8, 16, LANES), jnp.int32),
            vmem((2, 2, 8, 16, LANES), f32),
            vmem((XPEERS, PACKS, 8, LANES), f32),
            vmem((3, PACKS, 8, LANES), f32),
            vmem((PACKS, 8, LANES), f32),
            vmem((PACKS, 8, LANES), f32),
            vmem((2, 8, 16, 32), f32),
            dma((24,)),
            dma((2,)),
            dma((STEPS, 8)),
            dma((STEPS, 8)),
            dma((STEPS + 1, 4)),
            dma((STEPS + 1, 4)),
            dma((3, 2)),
            dma((3, 2)),
            dma,
            dma,
            pltpu.SemaphoreType.REGULAR,
        ],
        compiler_params=pltpu.CompilerParams(
            collective_id=0, has_side_effects=True, vmem_limit_bytes=24 << 20
        ),
    )(
        *(
            pltpu.with_memory_space_constraint(v, pltpu.HBM)
            for v in (
                adj_now, adj_later, forward_field, lame_first, shear, buoyancy, seafloor_depth,
                station_columns, jnp.transpose(station_traces, (1, 0, 2)),
            )
        )
    )


def solution(mesh):
    in_specs = (
        P("src", None, "tx", "ty", None),
        P("src", None, "tx", "ty", None),
        P("src", None, None, "tx", "ty", None),
        P("tx", "ty", None),
        P("tx", "ty", None),
        P("tx", "ty", None),
        P("tx", "ty"),
        P("src", None),
        P("src", None, None),
    )
    out_specs = (P("src", None, "tx", "ty", None), P(None, "tx", "ty", "src"))
    return jax.shard_map(body, mesh=mesh, in_specs=in_specs, out_specs=out_specs, check_vma=False)
```

```python
import functools

import jax
import jax.numpy as jnp
from jax import lax
from jax.experimental import pallas as pl
from jax.experimental.pallas import tpu as pltpu
from jax.sharding import PartitionSpec as P

STEPS = 3
TIME_SCALE = 0.04
MESH = pl.DeviceIdType.MESH
LANES = 128
PITCH = 32
FIRST = 8
XPEERS = 4
PACKS = 13
DIRS = ((-1, 0), (1, 0), (0, -1), (0, 1), (-1, -1), (-1, 1), (1, -1), (1, 1))


def opposite(d):
    return DIRS.index((-DIRS[d][0], -DIRS[d][1]))


def kernel(
    adj_now, adj_later, forward, lame, shear, buoyancy, seafloor, columns, traces,
    adj_out, kernels_out,
    u, now, prev, fin, fraw, fw, fx_land, fy_send, fy_land,
    y_send, y_land, c_send, c_land,
    p_lame, p_shear, p_buoy, p_sea, p_cols, p_traces,
    c_lap, c_div, q_add, sea_cols, acc, pack, x_land, z_send, z_land, kout,
    load_sem, out_sem, halo_send, halo_recv, fwd_send, fwd_recv, x_sem_s, x_sem_r, z_sem_s, z_sem_r, far_ready,
):
    tx, ty, src = lax.axis_index("tx"), lax.axis_index("ty"), lax.axis_index("src")
    ntx, nty = lax.axis_size("tx"), lax.axis_size("ty")
    half, xpos = src // XPEERS, lax.rem(src, XPEERS)

    def exists(d):
        dx, dy = DIRS[d]
        good = None
        for pos, step, count in ((tx, dx, ntx), (ty, dy, nty)):
            if step:
                here = (pos > 0) if step < 0 else (pos < count - 1)
                good = here if good is None else jnp.logical_and(good, here)
        return good

    def neighbour(d):
        dx, dy = DIRS[d]
        target = {}
        if dx:
            target["tx"] = tx + dx
        if dy:
            target["ty"] = ty + dy
        return target

    def src_peer(r):
        return {"src": half * XPEERS + lax.rem(xpos + r, XPEERS)}

    far = {"src": (1 - half) * XPEERS + xpos}

    loads = (
        (adj_now.at[0], now),
        (forward.at[0], fraw),
        (adj_later.at[0], prev),
        (lame, p_lame),
        (shear, p_shear),
        (buoyancy, p_buoy),
        (seafloor, p_sea),
        (columns, p_cols),
        (traces, p_traces),
    )
    copies = [pltpu.make_async_copy(a, b, load_sem.at[n]) for n, (a, b) in enumerate(loads)]

    barrier = pltpu.get_barrier_semaphore()
    expected = XPEERS - 1 + half
    for d in range(8):
        there = exists(d)
        expected = expected + there.astype(jnp.int32)

        @pl.when(there)
        def _(d=d):
            pl.semaphore_signal(barrier, inc=1, device_id=neighbour(d), device_id_type=MESH)

    for r in range(1, XPEERS):
        pl.semaphore_signal(barrier, inc=1, device_id=src_peer(r), device_id_type=MESH)

    @pl.when(half == 0)
    def _():
        pl.semaphore_signal(barrier, inc=1, device_id=far, device_id_type=MESH)

    copies[0].start()
    pl.semaphore_wait(barrier, expected)

    @pl.when(half == 1)
    def _():
        pl.semaphore_signal(far_ready, inc=1, device_id=far, device_id_type=MESH)


    def x_rows(t, plane):
        return u.at[t, :, :, pl.ds(plane * PITCH + FIRST, 16), :]

    def halo_source(t, d):
        if d == 0:
            return x_rows(t, 1)
        if d == 1:
            return x_rows(t, 8)
        if d < 4:
            return y_send.at[t, d - 2]
        return c_send.at[t, d - 4]

    def halo_target(t, d):
        if d == 0:
            return x_rows(t, 0)
        if d == 1:
            return x_rows(t, 9)
        if d < 4:
            return y_land.at[t, d - 2]
        return c_land.at[t, d - 4]

    def halo_copy(t, d, arrive):
        side = d if arrive else opposite(d)
        return pltpu.make_async_remote_copy(
            src_ref=halo_source(t, d),
            dst_ref=halo_target(t, side),
            send_sem=halo_send.at[t, d],
            recv_sem=halo_recv.at[t, side],
            device_id=neighbour(d),
            device_id_type=MESH,
        )

    def corner_row(d):
        dx, dy = DIRS[d]
        return (1 if dx < 0 else 8) * PITCH + (FIRST if dy < 0 else FIRST + 15)

    def start(t, directions):
        for d in directions:

            @pl.when(exists(d))
            def _(d=d):
                halo_copy(t, d, False).start()

    def send_corners(t):
        for d in range(4, 8):
            for k in range(2):
                for c in range(2):
                    row = corner_row(d)
                    c_send[t, d - 4, pl.ds(2 * k + c, 1), :] = u[t, k, c, pl.ds(row, 1), :]
        start(t, range(4, 8))

    def send_y(t):
        for k in range(3):
            for c in range(2):
                y_send[t, 0, k, c] = u[t, k, c, pl.ds(PITCH + FIRST, 8, stride=PITCH), :]
                y_send[t, 1, k, c] = u[t, k, c, pl.ds(PITCH + FIRST + 15, 8, stride=PITCH), :]
        start(t, range(2, 4))

    def receive_halo(t):
        for d in range(8):

            @pl.when(exists(d))
            def _(d=d):
                halo_copy(t, d, True).wait_recv()

        for k in range(3):
            for c in range(2):
                u[t, k, c, pl.ds(PITCH + FIRST - 1, 8, stride=PITCH), :] = y_land[t, 0, k, c]
                u[t, k, c, pl.ds(PITCH + FIRST + 16, 8, stride=PITCH), :] = y_land[t, 1, k, c]
        for d in range(4, 8):
            dx, dy = DIRS[d]
            row = (0 if dx < 0 else 9) * PITCH + (FIRST - 1 if dy < 0 else FIRST + 16)
            for k in range(2):
                for c in range(2):
                    u[t, k, c, pl.ds(row, 1), :] = c_land[t, d - 4, pl.ds(2 * k + c, 1), :]

    for d in range(2):

        @pl.when(exists(d))
        def _(d=d):
            side = opposite(d)
            for c in range(2):
                pltpu.make_async_remote_copy(
                    src_ref=adj_now.at[0, :, 7 * d, :, pl.ds(c * LANES, LANES)],
                    dst_ref=u.at[0, :, c, pl.ds((9 if side else 0) * PITCH + FIRST, 16), :],
                    send_sem=halo_send.at[0, d],
                    recv_sem=halo_recv.at[0, side],
                    device_id=neighbour(d),
                    device_id_type=MESH,
                ).start()

    for copy in copies[1:]:
        copy.start()

    def forward_copy(n, d, arrive):
        side = d if arrive else opposite(d)
        if n == 0:
            source, target = fraw.at[:, :, 7 * d], fx_land.at[side]
        else:
            source, target = fy_send.at[d - 2], fy_land.at[side - 2]
        return pltpu.make_async_remote_copy(
            src_ref=source,
            dst_ref=target,
            send_sem=fwd_send.at[n, d],
            recv_sem=fwd_recv.at[n, side],
            device_id=neighbour(d),
            device_id_type=MESH,
        )

    def each_forward(n, act):
        for d in (0, 1) if n == 0 else (2, 3):

            @pl.when(exists(d))
            def _(d=d):
                act(n, d)

    lane = lax.broadcasted_iota(jnp.int32, (16, LANES), 1)
    is_first, is_last = lane == 0, lane == LANES - 1

    def shift_z(pair):
        a, b = pair
        ua, ub = pltpu.roll(a, LANES - 1, 1), pltpu.roll(b, LANES - 1, 1)
        da, db = pltpu.roll(a, 1, 1), pltpu.roll(b, 1, 1)
        above = (jnp.where(is_last, ub, ua), jnp.where(is_last, 0.0, ub))
        below = (jnp.where(is_first, 0.0, da), jnp.where(is_first, da, db))
        return above, below

    def diff_z(pair):
        above, below = shift_z(pair)
        return [above[c] - below[c] for c in range(2)]

    copies[0].wait()
    for k in range(3):
        for x in range(8):
            for c in range(2):
                rows = now[k, x, :, c * LANES : (c + 1) * LANES]
                u[0, k, c, pl.ds((x + 1) * PITCH + FIRST, 16), :] = rows
    send_corners(0)
    send_y(0)
    copies[1].wait()
    each_forward(0, lambda n, d: forward_copy(n, d, False).start())

    zero = jnp.zeros((16, LANES), jnp.float32)
    for d in range(2):

        @pl.when(jnp.logical_not(exists(d)))
        def _(d=d):
            plane = 0 if d == 0 else 9
            for t in range(STEPS):
                for k in range(3):
                    for c in range(2):
                        u[t, k, c, pl.ds(plane * PITCH + FIRST, 16), :] = zero
            fx_land[d] = jnp.zeros(fx_land.shape[1:], fx_land.dtype)

    for d in range(2, 4):

        @pl.when(jnp.logical_not(exists(d)))
        def _(d=d):
            for t in range(STEPS):
                y_land[t, d - 2] = jnp.zeros(y_land.shape[2:], jnp.float32)
            fy_land[d - 2] = jnp.zeros(fy_land.shape[1:], fy_land.dtype)

    for d in range(4, 8):

        @pl.when(jnp.logical_not(exists(d)))
        def _(d=d):
            for t in range(STEPS):
                c_land[t, d - 4] = jnp.zeros(c_land.shape[2:], jnp.float32)


    def widen(n, carry):
        t, k = n // 3, lax.rem(n, 3)
        for x in range(8):
            rows = fraw[t, k, x].astype(jnp.float32)
            for c in range(2):
                fw[t, k, c, pl.ds((x + 1) * PITCH + FIRST, 16), :] = rows[:, c * LANES : (c + 1) * LANES]
        for c in range(2):
            for side in range(2):
                row = PITCH + FIRST + 15 * side
                fy_send[side, t, k, c] = fw[t, k, c, pl.ds(row, 8, stride=PITCH), :].astype(fy_send.dtype)
        return carry

    lax.fori_loop(0, 3 * STEPS, widen, 0)
    each_forward(1, lambda n, d: forward_copy(n, d, False).start())

    for copy in copies[2:]:
        copy.wait()
    sublane = lax.broadcasted_iota(jnp.int32, (16, 16), 0)
    sublane_lane = lax.broadcasted_iota(jnp.int32, (16, 16), 1)
    stations = p_cols.shape[1]
    y_of = lax.broadcasted_iota(jnp.int32, (16, stations), 0)
    total_y = 16 * nty

    def coefficients(x, carry):
        depth_row = jnp.broadcast_to(p_sea[pl.ds(x, 1), :].astype(jnp.float32), (16, 16))
        depth = jnp.sum(jnp.where(sublane == sublane_lane, depth_row, 0.0), axis=1, keepdims=True)
        depth = jnp.broadcast_to(depth, (16, LANES)).astype(jnp.int32)
        sea_cols[x] = depth
        column = (tx * 8 + x) * total_y + ty * 16 + y_of
        hit = jnp.broadcast_to(p_cols[...], (16, stations)) == column
        amps = []
        for t in range(STEPS):
            amp = jnp.broadcast_to(p_traces[t], (16, stations))
            amp = jnp.sum(jnp.where(hit, amp, 0.0), axis=1, keepdims=True)
            amps.append(jnp.broadcast_to(amp, (16, LANES)))
        for c in range(2):
            zs = slice(c * LANES, (c + 1) * LANES)
            scaled = TIME_SCALE * p_buoy[x, :, zs]
            level = lane + c * LANES
            mu = jnp.where(level >= depth, p_shear[x, :, zs], 0.0)
            c_lap[c, x] = scaled * mu
            c_div[c, x] = scaled * (p_lame[x, :, zs] + mu)
            for t in range(STEPS):
                q_add[t, c, x] = jnp.where(level == depth, scaled * amps[t], 0.0)
        return carry

    lax.fori_loop(0, 8, coefficients, 0)

    def step(t, first, count, stride):
        def row(i, carry):
            x = first + i * stride
            base = (x + 1) * PITCH + FIRST

            def at(k, c, dx, dy):
                return u[t, k, c, pl.ds(base + dx * PITCH + dy, 16), :]

            both = range(2)
            centre = [[at(k, c, 0, 0) for c in both] for k in range(3)]
            gx, gy, fresh = [], [], []
            lap, second = [], []
            for k in range(3):
                xp, xm = [at(k, c, 1, 0) for c in both], [at(k, c, -1, 0) for c in both]
                yp, ym = [at(k, c, 0, 1) for c in both], [at(k, c, 0, -1) for c in both]
                zp, zm = shift_z(centre[k])
                gx.append([xp[c] - xm[c] for c in both])
                gy.append([yp[c] - ym[c] for c in both])
                sums = [[a[c] + b[c] for c in both] for a, b in ((xp, xm), (yp, ym), (zp, zm))]
                lap.append([sums[0][c] + sums[1][c] + sums[2][c] - 6.0 * centre[k][c] for c in both])
                second.append([sums[k][c] - 2.0 * centre[k][c] for c in both])

            def cross(k):
                return [
                    (at(k, c, 1, 1) - at(k, c, -1, 1)) - (at(k, c, 1, -1) - at(k, c, -1, -1)) for c in both
                ]

            cross_0, cross_1 = cross(0), cross(1)
            dz_gx2, dz_gy2 = diff_z(gx[2]), diff_z(gy[2])
            dz_mix = diff_z([gx[0][c] + gy[1][c] for c in both])
            mixed = [
                [cross_1[c] + dz_gx2[c] for c in both],
                [cross_0[c] + dz_gy2[c] for c in both],
                dz_mix,
            ]
            for k in range(3):
                for c in both:
                    if t == 0:
                        old = prev[k, x, :, c * LANES : (c + 1) * LANES]
                    else:
                        old = u[t - 1, k, c, pl.ds(base, 16), :]
                    new = (
                        (2.0 * centre[k][c] - old)
                        + c_lap[c, x] * lap[k][c]
                        + c_div[c, x] * (second[k][c] + 0.25 * mixed[k][c])
                    )
                    if k == 2:
                        new = new + q_add[t, c, x]
                    if t < STEPS - 1:
                        u[t + 1, k, c, pl.ds(base, 16), :] = new
                    else:
                        fin[k, x, :, c * LANES : (c + 1) * LANES] = new
            return carry

        lax.fori_loop(0, count, row, 0, unroll=2)

    def receive_forward(t):
        if t == 0:
            for n in range(2):
                each_forward(n, lambda n, d: forward_copy(n, d, True).wait_recv())
        for k in range(3):
            for side in range(2):
                plane = 9 * side
                rows = fx_land[side, t, k].astype(jnp.float32)
                for c in range(2):
                    fw[t, k, c, pl.ds(plane * PITCH + FIRST, 16), :] = rows[:, c * LANES : (c + 1) * LANES]
                    row = PITCH + (FIRST - 1 if side == 0 else FIRST + 16)
                    fw[t, k, c, pl.ds(row, 8, stride=PITCH), :] = fy_land[side, t, k, c].astype(jnp.float32)

    def diff_z_half(a, b, c):
        if c == 0:
            above = jnp.where(is_last, pltpu.roll(b, LANES - 1, 1), pltpu.roll(a, LANES - 1, 1))
            below = jnp.where(is_first, 0.0, pltpu.roll(a, 1, 1))
        else:
            above = jnp.where(is_last, 0.0, pltpu.roll(b, LANES - 1, 1))
            below = jnp.where(is_first, pltpu.roll(a, 1, 1), pltpu.roll(b, 1, 1))
        return above - below

    def accumulate(t, both=(0, 1)):
        def row(x, carry):
            base = (x + 1) * PITCH + FIRST

            def gradient(ref, k):
                at = lambda c, dx, dy: ref[t, k, c, pl.ds(base + dx * PITCH + dy, 16), :]
                g_x = {c: at(c, 1, 0) - at(c, -1, 0) for c in both}
                g_y = {c: at(c, 0, 1) - at(c, 0, -1) for c in both}
                pair = [at(c, 0, 0) for c in range(2)]
                if len(both) == 2:
                    g_z = diff_z(pair)
                else:
                    g_z = {both[0]: diff_z_half(*pair, both[0])}
                return g_x, g_y, g_z

            mu = div_u = div_f = None
            for k in range(3):
                gu, gf = gradient(u, k), gradient(fw, k)
                for d in range(3):
                    term = {c: gu[d][c] * gf[d][c] for c in both}
                    mu = term if mu is None else {c: mu[c] + term[c] for c in both}
                div_u = gu[k] if div_u is None else {c: div_u[c] + gu[k][c] for c in both}
                div_f = gf[k] if div_f is None else {c: div_f[c] + gf[k][c] for c in both}
            for c in both:
                lam = div_u[c] * div_f[c]
                if t == 0:
                    acc[0, c, x], acc[1, c, x] = lam, mu[c]
                else:
                    acc[0, c, x] = acc[0, c, x] + lam
                    acc[1, c, x] = acc[1, c, x] + mu[c]
            return carry

        lax.fori_loop(0, 8, row, 0, unroll=2)

    receive_halo(0)
    for t in range(STEPS - 1):
        step(t, 0, 2, 7)
        start(t + 1, range(2))
        send_corners(t + 1)
        step(t, 1, 6, 1)
        send_y(t + 1)
        receive_forward(t)
        accumulate(t)
        receive_halo(t + 1)
    lane8 = lax.broadcasted_iota(jnp.int32, (8, LANES), 1)
    even = lax.rem(lane8 // 32, 2) == 0
    low = lane8 < 64

    def quarters(v):
        w = []
        for a, b in ((v[0], v[1]), (v[2], v[3])):
            w.append(
                (
                    jnp.where(even, a, pltpu.roll(b, 32, 1)),
                    jnp.where(even, pltpu.roll(a, 96, 1), b),
                )
            )
        out = [None] * 4
        for odd in range(2):
            a, b = w[0][odd], w[1][odd]
            out[odd] = jnp.where(low, a, pltpu.roll(b, 64, 1))
            out[2 + odd] = jnp.where(low, pltpu.roll(a, 64, 1), b)
        return out

    def masked_mu(c, x, ys):
        return jnp.where(lane8 + c * LANES >= sea_cols[x, ys], acc[1, c, x, ys], 0.0)

    parts = ((0, 5), (5, 8))

    def fill(c):
        for s in range(2):
            ys = pl.ds(8 * s, 8)
            for g in range(2):
                n = parts[c][0] + 2 * s + g
                for q, tile in enumerate(quarters([acc[0, c, 4 * g + a, ys] for a in range(4)])):
                    pack[q, n] = tile
                if c == 1:
                    for q, tile in enumerate(quarters([masked_mu(1, 4 * g + a, ys) for a in range(4)])):
                        pack[q, n + 4] = tile
        if c == 0:
            rest = None
            for x in range(8):
                for s in range(2):
                    tile = masked_mu(0, x, pl.ds(8 * s, 8))
                    tile = pltpu.roll(tile, (2 * (2 * x + s) + 2) % LANES, 1)
                    rest = tile if rest is None else rest + tile
            for q in range(XPEERS):
                pack[q, 4] = rest

    def x_copy(r, c):
        rows = pl.ds(*parts[c])
        return pltpu.make_async_remote_copy(
            src_ref=pack.at[lax.rem(xpos + r, XPEERS), rows],
            dst_ref=x_land.at[r - 1, rows],
            send_sem=x_sem_s.at[r - 1, c],
            recv_sem=x_sem_r.at[r - 1, c],
            device_id=src_peer(r),
            device_id_type=MESH,
        )

    def x_total(c):
        for r in (1, 3, 2):
            x_copy(r, c).wait_recv()
        for n in range(parts[c][0], sum(parts[c])):
            z_send[n] = pack[xpos, n] + x_land[0, n] + x_land[1, n] + x_land[2, n]

    def z_copy(c):
        rows = pl.ds(*parts[c])
        return pltpu.make_async_remote_copy(
            src_ref=z_send.at[rows],
            dst_ref=z_land.at[rows],
            send_sem=z_sem_s,
            recv_sem=z_sem_r,
            device_id=far,
            device_id_type=MESH,
        )

    receive_forward(STEPS - 1)
    for mine in range(2):

        @pl.when(half == mine)
        def _(mine=mine):
            for c in (1 - mine, mine):
                accumulate(STEPS - 1, (c,))
                fill(c)
                for r in (2, 1, 3):
                    x_copy(r, c).start()
            x_total(1 - mine)
            if mine == 0:
                pl.semaphore_wait(far_ready, 1)
            z_copy(1 - mine).start()

    step(STEPS - 1, 0, 8, 1)
    final_copy = pltpu.make_async_copy(fin, adj_out.at[0], out_sem.at[0])
    final_copy.start()

    for t in range(STEPS):
        for d in range(8):

            @pl.when(exists(d))
            def _(t=t, d=d):
                halo_copy(t, d, False).wait_send()

    for n in range(2):
        each_forward(n, lambda n, d: forward_copy(n, d, False).wait_send())
    for r in range(1, XPEERS):
        for c in range(2):
            x_copy(r, c).wait_send()

    scale = 0.25 / lax.axis_size("src")

    def unpack(kind, n, tile):
        s, g = n // 2, n % 2
        for a in range(4):
            part = pltpu.roll(tile, (LANES - 32 * a) % LANES, 1) if a else tile
            kout[kind, 4 * g + a, pl.ds(8 * s, 8), :] = part[:, :32]

    @pl.when(half == 0)
    def _():
        x_total(0)
        z_copy(0).wait_recv()
        for n in range(4):
            unpack(0, n, (z_send[n] + z_land[n]) * scale)
        rest = jnp.where(xpos == XPEERS - 1, (z_send[4] + z_land[4]) * scale, 0.0)
        tail = jnp.logical_and(lane8 >= 30, lane8 < 32)
        for x in range(8):
            for s in range(2):
                tile = pltpu.roll(rest, (30 - 2 * (2 * x + s)) % LANES, 1)
                kout[1, x, pl.ds(8 * s, 8), :] = jnp.where(tail, tile, 0.0)[:, :32]

    @pl.when(half == 1)
    def _():
        x_total(1)
        z_copy(1).wait_recv()
        for kind in range(2):
            for n in range(4):
                m = 5 + 4 * kind + n
                unpack(kind, n, (z_send[m] + z_land[m]) * scale)

    kernels_copy = pltpu.make_async_copy(kout, kernels_out, out_sem.at[1])
    kernels_copy.start()

    @pl.when(half == 0)
    def _():
        z_copy(1).wait_send()

    @pl.when(half == 1)
    def _():
        z_copy(0).wait_send()

    final_copy.wait()
    kernels_copy.wait()


def body(adj_now, adj_later, forward_field, lame_first, shear, buoyancy, seafloor_depth, station_columns, station_traces):
    f32, bf16 = jnp.float32, jnp.bfloat16
    vmem, dma = pltpu.VMEM, pltpu.SemaphoreType.DMA
    stations = station_columns.shape[1]
    anywhere = pl.BlockSpec(memory_space=pltpu.HBM)
    rows = 10 * PITCH
    return pl.pallas_call(
        kernel,
        name="adjoint",
        out_shape=(
            jax.ShapeDtypeStruct((1, 3, 8, 16, 256), f32),
            jax.ShapeDtypeStruct((2, 8, 16, 32), f32),
        ),
        in_specs=[anywhere] * 9,
        out_specs=(anywhere, anywhere),
        scratch_shapes=[
            vmem((STEPS, 3, 2, rows, LANES), f32),
            vmem((3, 8, 16, 256), f32),
            vmem((3, 8, 16, 256), f32),
            vmem((3, 8, 16, 256), f32),
            vmem((STEPS, 3, 8, 16, 256), bf16),
            vmem((STEPS, 3, 2, rows, LANES), f32),
            vmem((2, STEPS, 3, 16, 256), bf16),
            vmem((2, STEPS, 3, 2, 8, LANES), bf16),
            vmem((2, STEPS, 3, 2, 8, LANES), bf16),
            vmem((STEPS, 2, 3, 2, 8, LANES), f32),
            vmem((STEPS, 2, 3, 2, 8, LANES), f32),
            vmem((STEPS, 4, 4, LANES), f32),
            vmem((STEPS, 4, 4, LANES), f32),
            vmem((8, 16, 256), f32),
            vmem((8, 16, 256), f32),
            vmem((8, 16, 256), f32),
            vmem((8, 16), jnp.int32),
            vmem((1, stations), jnp.int32),
            vmem((STEPS, 1, stations), f32),
            vmem((2, 8, 16, LANES), f32),
            vmem((2, 8, 16, LANES), f32),
            vmem((STEPS, 2, 8, 16, LANES), f32),
            vmem((8, 16, LANES), jnp.int32),
            vmem((2, 2, 8, 16, LANES), f32),
            vmem((XPEERS, PACKS, 8, LANES), f32),
            vmem((3, PACKS, 8, LANES), f32),
            vmem((PACKS, 8, LANES), f32),
            vmem((PACKS, 8, LANES), f32),
            vmem((2, 8, 16, 32), f32),
            dma((9,)),
            dma((2,)),
            dma((STEPS, 8)),
            dma((STEPS, 8)),
            dma((2, 4)),
            dma((2, 4)),
            dma((3, 2)),
            dma((3, 2)),
            dma,
            dma,
            pltpu.SemaphoreType.REGULAR,
        ],
        compiler_params=pltpu.CompilerParams(
            collective_id=0, has_side_effects=True, vmem_limit_bytes=24 << 20
        ),
    )(
        *(
            pltpu.with_memory_space_constraint(v, pltpu.HBM)
            for v in (
                adj_now, adj_later, forward_field, lame_first, shear, buoyancy, seafloor_depth,
                station_columns, jnp.transpose(station_traces, (1, 0, 2)),
            )
        )
    )


def solution(mesh):
    in_specs = (
        P("src", None, "tx", "ty", None),
        P("src", None, "tx", "ty", None),
        P("src", None, None, "tx", "ty", None),
        P("tx", "ty", None),
        P("tx", "ty", None),
        P("tx", "ty", None),
        P("tx", "ty"),
        P("src", None),
        P("src", None, None),
    )
    out_specs = (P("src", None, "tx", "ty", None), P(None, "tx", "ty", "src"))
    return jax.shard_map(body, mesh=mesh, in_specs=in_specs, out_specs=out_specs, check_vma=False)
```

```python
import functools

import jax
import jax.numpy as jnp
from jax import lax
from jax.experimental import pallas as pl
from jax.experimental.pallas import tpu as pltpu
from jax.sharding import PartitionSpec as P

STEPS = 3
TIME_SCALE = 0.04
MESH = pl.DeviceIdType.MESH
LANES = 128
PITCH = 32
FIRST = 8
XPEERS = 4
PACKS = 13
DIRS = ((-1, 0), (1, 0), (0, -1), (0, 1), (-1, -1), (-1, 1), (1, -1), (1, 1))


def opposite(d):
    return DIRS.index((-DIRS[d][0], -DIRS[d][1]))


def kernel(
    adj_now, adj_later, forward, lame, shear, buoyancy, seafloor, columns, traces,
    adj_out, kernels_out,
    u, now, prev, fin, fraw, fw, fx_land, fy_send, fy_land,
    y_send, y_land, c_send, c_land,
    p_lame, p_shear, p_buoy, p_sea, p_cols, p_traces,
    c_lap, c_div, q_add, sea_cols, acc, pack, x_land, z_send, z_land, kout,
    load_sem, out_sem, halo_send, halo_recv, fwd_send, fwd_recv, x_sem_s, x_sem_r, z_sem_s, z_sem_r, far_ready,
):
    tx, ty, src = lax.axis_index("tx"), lax.axis_index("ty"), lax.axis_index("src")
    ntx, nty = lax.axis_size("tx"), lax.axis_size("ty")
    half, xpos = src // XPEERS, lax.rem(src, XPEERS)

    def exists(d):
        dx, dy = DIRS[d]
        good = None
        for pos, step, count in ((tx, dx, ntx), (ty, dy, nty)):
            if step:
                here = (pos > 0) if step < 0 else (pos < count - 1)
                good = here if good is None else jnp.logical_and(good, here)
        return good

    def neighbour(d):
        dx, dy = DIRS[d]
        target = {}
        if dx:
            target["tx"] = tx + dx
        if dy:
            target["ty"] = ty + dy
        return target

    def src_peer(r):
        return {"src": half * XPEERS + lax.rem(xpos + r, XPEERS)}

    far = {"src": (1 - half) * XPEERS + xpos}

    loads = (
        (adj_now.at[0], now),
        (forward.at[0], fraw),
        (adj_later.at[0], prev),
        (lame, p_lame),
        (shear, p_shear),
        (buoyancy, p_buoy),
        (seafloor, p_sea),
        (columns, p_cols),
        (traces, p_traces),
    )
    copies = [pltpu.make_async_copy(a, b, load_sem.at[n]) for n, (a, b) in enumerate(loads)]
    copies[0].start()

    barrier = pltpu.get_barrier_semaphore()
    expected = XPEERS - 1 + half
    for d in range(8):
        there = exists(d)
        expected = expected + there.astype(jnp.int32)

        @pl.when(there)
        def _(d=d):
            pl.semaphore_signal(barrier, inc=1, device_id=neighbour(d), device_id_type=MESH)

    for r in range(1, XPEERS):
        pl.semaphore_signal(barrier, inc=1, device_id=src_peer(r), device_id_type=MESH)

    @pl.when(half == 0)
    def _():
        pl.semaphore_signal(barrier, inc=1, device_id=far, device_id_type=MESH)

    pl.semaphore_wait(barrier, expected)

    @pl.when(half == 1)
    def _():
        pl.semaphore_signal(far_ready, inc=1, device_id=far, device_id_type=MESH)


    def x_rows(t, plane):
        return u.at[t, :, :, pl.ds(plane * PITCH + FIRST, 16), :]

    def halo_source(t, d):
        if d == 0:
            return x_rows(t, 1)
        if d == 1:
            return x_rows(t, 8)
        if d < 4:
            return y_send.at[t, d - 2]
        return c_send.at[t, d - 4]

    def halo_target(t, d):
        if d == 0:
            return x_rows(t, 0)
        if d == 1:
            return x_rows(t, 9)
        if d < 4:
            return y_land.at[t, d - 2]
        return c_land.at[t, d - 4]

    def halo_copy(t, d, arrive):
        side = d if arrive else opposite(d)
        return pltpu.make_async_remote_copy(
            src_ref=halo_source(t, d),
            dst_ref=halo_target(t, side),
            send_sem=halo_send.at[t, d],
            recv_sem=halo_recv.at[t, side],
            device_id=neighbour(d),
            device_id_type=MESH,
        )

    def corner_row(d):
        dx, dy = DIRS[d]
        return (1 if dx < 0 else 8) * PITCH + (FIRST if dy < 0 else FIRST + 15)

    def start(t, directions):
        for d in directions:

            @pl.when(exists(d))
            def _(d=d):
                halo_copy(t, d, False).start()

    def send_corners(t):
        for d in range(4, 8):
            for k in range(2):
                for c in range(2):
                    row = corner_row(d)
                    c_send[t, d - 4, pl.ds(2 * k + c, 1), :] = u[t, k, c, pl.ds(row, 1), :]
        start(t, range(4, 8))

    def send_y(t):
        for k in range(3):
            for c in range(2):
                y_send[t, 0, k, c] = u[t, k, c, pl.ds(PITCH + FIRST, 8, stride=PITCH), :]
                y_send[t, 1, k, c] = u[t, k, c, pl.ds(PITCH + FIRST + 15, 8, stride=PITCH), :]
        start(t, range(2, 4))

    def receive_halo(t):
        for d in range(8):

            @pl.when(exists(d))
            def _(d=d):
                halo_copy(t, d, True).wait_recv()

        for k in range(3):
            for c in range(2):
                u[t, k, c, pl.ds(PITCH + FIRST - 1, 8, stride=PITCH), :] = y_land[t, 0, k, c]
                u[t, k, c, pl.ds(PITCH + FIRST + 16, 8, stride=PITCH), :] = y_land[t, 1, k, c]
        for d in range(4, 8):
            dx, dy = DIRS[d]
            row = (0 if dx < 0 else 9) * PITCH + (FIRST - 1 if dy < 0 else FIRST + 16)
            for k in range(2):
                for c in range(2):
                    u[t, k, c, pl.ds(row, 1), :] = c_land[t, d - 4, pl.ds(2 * k + c, 1), :]

    for d in range(2):

        @pl.when(exists(d))
        def _(d=d):
            side = opposite(d)
            for c in range(2):
                pltpu.make_async_remote_copy(
                    src_ref=adj_now.at[0, :, 7 * d, :, pl.ds(c * LANES, LANES)],
                    dst_ref=u.at[0, :, c, pl.ds((9 if side else 0) * PITCH + FIRST, 16), :],
                    send_sem=halo_send.at[0, d],
                    recv_sem=halo_recv.at[0, side],
                    device_id=neighbour(d),
                    device_id_type=MESH,
                ).start()

    for copy in copies[1:]:
        copy.start()

    def forward_copy(n, d, arrive):
        side = d if arrive else opposite(d)
        if n != 1:
            steps = pl.ds(0, 1) if n == 0 else pl.ds(1, STEPS - 1)
            source, target = fraw.at[steps, :, 7 * d], fx_land.at[side, steps]
        else:
            source, target = fy_send.at[d - 2], fy_land.at[side - 2]
        return pltpu.make_async_remote_copy(
            src_ref=source,
            dst_ref=target,
            send_sem=fwd_send.at[n, d],
            recv_sem=fwd_recv.at[n, side],
            device_id=neighbour(d),
            device_id_type=MESH,
        )

    def each_forward(n, act):
        for d in (2, 3) if n == 1 else (0, 1):

            @pl.when(exists(d))
            def _(d=d):
                act(n, d)

    lane = lax.broadcasted_iota(jnp.int32, (16, LANES), 1)
    is_first, is_last = lane == 0, lane == LANES - 1

    def shift_z(pair):
        a, b = pair
        ua, ub = pltpu.roll(a, LANES - 1, 1), pltpu.roll(b, LANES - 1, 1)
        da, db = pltpu.roll(a, 1, 1), pltpu.roll(b, 1, 1)
        above = (jnp.where(is_last, ub, ua), jnp.where(is_last, 0.0, ub))
        below = (jnp.where(is_first, 0.0, da), jnp.where(is_first, da, db))
        return above, below

    def diff_z(pair):
        above, below = shift_z(pair)
        return [above[c] - below[c] for c in range(2)]

    copies[0].wait()
    for k in range(3):
        for x in range(8):
            for c in range(2):
                rows = now[k, x, :, c * LANES : (c + 1) * LANES]
                u[0, k, c, pl.ds((x + 1) * PITCH + FIRST, 16), :] = rows
    send_corners(0)
    send_y(0)
    copies[1].wait()
    each_forward(0, lambda n, d: forward_copy(n, d, False).start())

    zero = jnp.zeros((16, LANES), jnp.float32)
    for d in range(2):

        @pl.when(jnp.logical_not(exists(d)))
        def _(d=d):
            plane = 0 if d == 0 else 9
            for t in range(STEPS):
                for k in range(3):
                    for c in range(2):
                        u[t, k, c, pl.ds(plane * PITCH + FIRST, 16), :] = zero
            fx_land[d] = jnp.zeros(fx_land.shape[1:], fx_land.dtype)

    for d in range(2, 4):

        @pl.when(jnp.logical_not(exists(d)))
        def _(d=d):
            for t in range(STEPS):
                y_land[t, d - 2] = jnp.zeros(y_land.shape[2:], jnp.float32)
            fy_land[d - 2] = jnp.zeros(fy_land.shape[1:], fy_land.dtype)

    for d in range(4, 8):

        @pl.when(jnp.logical_not(exists(d)))
        def _(d=d):
            for t in range(STEPS):
                c_land[t, d - 4] = jnp.zeros(c_land.shape[2:], jnp.float32)


    def widen(n, carry):
        t, k = n // 3, lax.rem(n, 3)
        for x in range(8):
            rows = fraw[t, k, x].astype(jnp.float32)
            for c in range(2):
                fw[t, k, c, pl.ds((x + 1) * PITCH + FIRST, 16), :] = rows[:, c * LANES : (c + 1) * LANES]
        for c in range(2):
            for side in range(2):
                row = PITCH + FIRST + 15 * side
                fy_send[side, t, k, c] = fw[t, k, c, pl.ds(row, 8, stride=PITCH), :].astype(fy_send.dtype)
        return carry

    lax.fori_loop(0, 3 * STEPS, widen, 0)
    each_forward(1, lambda n, d: forward_copy(n, d, False).start())

    for copy in copies[2:]:
        copy.wait()
    sublane = lax.broadcasted_iota(jnp.int32, (16, 16), 0)
    sublane_lane = lax.broadcasted_iota(jnp.int32, (16, 16), 1)
    stations = p_cols.shape[1]
    y_of = lax.broadcasted_iota(jnp.int32, (16, stations), 0)
    total_y = 16 * nty

    def coefficients(x, carry):
        depth_row = jnp.broadcast_to(p_sea[pl.ds(x, 1), :].astype(jnp.float32), (16, 16))
        depth = jnp.sum(jnp.where(sublane == sublane_lane, depth_row, 0.0), axis=1, keepdims=True)
        depth = jnp.broadcast_to(depth, (16, LANES)).astype(jnp.int32)
        sea_cols[x] = depth
        column = (tx * 8 + x) * total_y + ty * 16 + y_of
        hit = jnp.broadcast_to(p_cols[...], (16, stations)) == column
        amps = []
        for t in range(STEPS):
            amp = jnp.broadcast_to(p_traces[t], (16, stations))
            amp = jnp.sum(jnp.where(hit, amp, 0.0), axis=1, keepdims=True)
            amps.append(jnp.broadcast_to(amp, (16, LANES)))
        for c in range(2):
            zs = slice(c * LANES, (c + 1) * LANES)
            scaled = TIME_SCALE * p_buoy[x, :, zs]
            level = lane + c * LANES
            mu = jnp.where(level >= depth, p_shear[x, :, zs], 0.0)
            c_lap[c, x] = scaled * mu
            c_div[c, x] = scaled * (p_lame[x, :, zs] + mu)
            for t in range(STEPS):
                q_add[t, c, x] = jnp.where(level == depth, scaled * amps[t], 0.0)
        return carry

    lax.fori_loop(0, 8, coefficients, 0)

    def step(t, first, count, stride):
        def row(i, carry):
            x = first + i * stride
            base = (x + 1) * PITCH + FIRST

            def at(k, c, dx, dy):
                return u[t, k, c, pl.ds(base + dx * PITCH + dy, 16), :]

            both = range(2)
            centre = [[at(k, c, 0, 0) for c in both] for k in range(3)]
            gx, gy, fresh = [], [], []
            lap, second = [], []
            for k in range(3):
                xp, xm = [at(k, c, 1, 0) for c in both], [at(k, c, -1, 0) for c in both]
                yp, ym = [at(k, c, 0, 1) for c in both], [at(k, c, 0, -1) for c in both]
                zp, zm = shift_z(centre[k])
                gx.append([xp[c] - xm[c] for c in both])
                gy.append([yp[c] - ym[c] for c in both])
                sums = [[a[c] + b[c] for c in both] for a, b in ((xp, xm), (yp, ym), (zp, zm))]
                lap.append([sums[0][c] + sums[1][c] + sums[2][c] - 6.0 * centre[k][c] for c in both])
                second.append([sums[k][c] - 2.0 * centre[k][c] for c in both])

            def cross(k):
                return [
                    (at(k, c, 1, 1) - at(k, c, -1, 1)) - (at(k, c, 1, -1) - at(k, c, -1, -1)) for c in both
                ]

            cross_0, cross_1 = cross(0), cross(1)
            dz_gx2, dz_gy2 = diff_z(gx[2]), diff_z(gy[2])
            dz_mix = diff_z([gx[0][c] + gy[1][c] for c in both])
            mixed = [
                [cross_1[c] + dz_gx2[c] for c in both],
                [cross_0[c] + dz_gy2[c] for c in both],
                dz_mix,
            ]
            for k in range(3):
                for c in both:
                    if t == 0:
                        old = prev[k, x, :, c * LANES : (c + 1) * LANES]
                    else:
                        old = u[t - 1, k, c, pl.ds(base, 16), :]
                    new = (
                        (2.0 * centre[k][c] - old)
                        + c_lap[c, x] * lap[k][c]
                        + c_div[c, x] * (second[k][c] + 0.25 * mixed[k][c])
                    )
                    if k == 2:
                        new = new + q_add[t, c, x]
                    if t < STEPS - 1:
                        u[t + 1, k, c, pl.ds(base, 16), :] = new
                    else:
                        fin[k, x, :, c * LANES : (c + 1) * LANES] = new
            return carry

        lax.fori_loop(0, count, row, 0, unroll=2)

    def receive_forward(t):
        for n in ((0, 1), (2,), ())[t]:
            each_forward(n, lambda n, d: forward_copy(n, d, True).wait_recv())
        for k in range(3):
            for side in range(2):
                plane = 9 * side
                rows = fx_land[side, t, k].astype(jnp.float32)
                for c in range(2):
                    fw[t, k, c, pl.ds(plane * PITCH + FIRST, 16), :] = rows[:, c * LANES : (c + 1) * LANES]
                    row = PITCH + (FIRST - 1 if side == 0 else FIRST + 16)
                    fw[t, k, c, pl.ds(row, 8, stride=PITCH), :] = fy_land[side, t, k, c].astype(jnp.float32)

    def diff_z_half(a, b, c):
        if c == 0:
            above = jnp.where(is_last, pltpu.roll(b, LANES - 1, 1), pltpu.roll(a, LANES - 1, 1))
            below = jnp.where(is_first, 0.0, pltpu.roll(a, 1, 1))
        else:
            above = jnp.where(is_last, 0.0, pltpu.roll(b, LANES - 1, 1))
            below = jnp.where(is_first, pltpu.roll(a, 1, 1), pltpu.roll(b, 1, 1))
        return above - below

    def accumulate(t, both=(0, 1)):
        def row(x, carry):
            base = (x + 1) * PITCH + FIRST

            def gradient(ref, k):
                at = lambda c, dx, dy: ref[t, k, c, pl.ds(base + dx * PITCH + dy, 16), :]
                g_x = {c: at(c, 1, 0) - at(c, -1, 0) for c in both}
                g_y = {c: at(c, 0, 1) - at(c, 0, -1) for c in both}
                pair = [at(c, 0, 0) for c in range(2)]
                if len(both) == 2:
                    g_z = diff_z(pair)
                else:
                    g_z = {both[0]: diff_z_half(*pair, both[0])}
                return g_x, g_y, g_z

            mu = div_u = div_f = None
            for k in range(3):
                gu, gf = gradient(u, k), gradient(fw, k)
                for d in range(3):
                    term = {c: gu[d][c] * gf[d][c] for c in both}
                    mu = term if mu is None else {c: mu[c] + term[c] for c in both}
                div_u = gu[k] if div_u is None else {c: div_u[c] + gu[k][c] for c in both}
                div_f = gf[k] if div_f is None else {c: div_f[c] + gf[k][c] for c in both}
            for c in both:
                lam = div_u[c] * div_f[c]
                if t == 0:
                    acc[0, c, x], acc[1, c, x] = lam, mu[c]
                else:
                    acc[0, c, x] = acc[0, c, x] + lam
                    acc[1, c, x] = acc[1, c, x] + mu[c]
            return carry

        lax.fori_loop(0, 8, row, 0, unroll=2)

    receive_halo(0)
    for t in range(STEPS - 1):
        step(t, 0, 2, 7)
        start(t + 1, range(2))
        send_corners(t + 1)
        step(t, 1, 6, 1)
        send_y(t + 1)
        if t == 0:
            each_forward(2, lambda n, d: forward_copy(n, d, False).start())
        receive_forward(t)
        accumulate(t)
        receive_halo(t + 1)
    lane8 = lax.broadcasted_iota(jnp.int32, (8, LANES), 1)
    even = lax.rem(lane8 // 32, 2) == 0
    low = lane8 < 64

    def quarters(v):
        w = []
        for a, b in ((v[0], v[1]), (v[2], v[3])):
            w.append(
                (
                    jnp.where(even, a, pltpu.roll(b, 32, 1)),
                    jnp.where(even, pltpu.roll(a, 96, 1), b),
                )
            )
        out = [None] * 4
        for odd in range(2):
            a, b = w[0][odd], w[1][odd]
            out[odd] = jnp.where(low, a, pltpu.roll(b, 64, 1))
            out[2 + odd] = jnp.where(low, pltpu.roll(a, 64, 1), b)
        return out

    def masked_mu(c, x, ys):
        return jnp.where(lane8 + c * LANES >= sea_cols[x, ys], acc[1, c, x, ys], 0.0)

    parts = ((0, 5), (5, 8))

    def fill(c):
        for s in range(2):
            ys = pl.ds(8 * s, 8)
            for g in range(2):
                n = parts[c][0] + 2 * s + g
                for q, tile in enumerate(quarters([acc[0, c, 4 * g + a, ys] for a in range(4)])):
                    pack[q, n] = tile
                if c == 1:
                    for q, tile in enumerate(quarters([masked_mu(1, 4 * g + a, ys) for a in range(4)])):
                        pack[q, n + 4] = tile
        if c == 0:
            rest = None
            for x in range(8):
                for s in range(2):
                    tile = masked_mu(0, x, pl.ds(8 * s, 8))
                    tile = pltpu.roll(tile, (2 * (2 * x + s) + 2) % LANES, 1)
                    rest = tile if rest is None else rest + tile
            for q in range(XPEERS):
                pack[q, 4] = rest

    def x_copy(r, c):
        rows = pl.ds(*parts[c])
        return pltpu.make_async_remote_copy(
            src_ref=pack.at[lax.rem(xpos + r, XPEERS), rows],
            dst_ref=x_land.at[r - 1, rows],
            send_sem=x_sem_s.at[r - 1, c],
            recv_sem=x_sem_r.at[r - 1, c],
            device_id=src_peer(r),
            device_id_type=MESH,
        )

    def x_total(c):
        for r in (1, 3, 2):
            x_copy(r, c).wait_recv()
        for n in range(parts[c][0], sum(parts[c])):
            z_send[n] = pack[xpos, n] + x_land[0, n] + x_land[1, n] + x_land[2, n]

    def z_copy(c):
        rows = pl.ds(*parts[c])
        return pltpu.make_async_remote_copy(
            src_ref=z_send.at[rows],
            dst_ref=z_land.at[rows],
            send_sem=z_sem_s,
            recv_sem=z_sem_r,
            device_id=far,
            device_id_type=MESH,
        )

    receive_forward(STEPS - 1)
    for mine in range(2):

        @pl.when(half == mine)
        def _(mine=mine):
            for c in (1 - mine, mine):
                accumulate(STEPS - 1, (c,))
                fill(c)
                for r in (2, 1, 3):
                    x_copy(r, c).start()
            x_total(1 - mine)
            if mine == 0:
                pl.semaphore_wait(far_ready, 1)
            z_copy(1 - mine).start()

    step(STEPS - 1, 0, 8, 1)
    final_copy = pltpu.make_async_copy(fin, adj_out.at[0], out_sem.at[0])
    final_copy.start()

    for t in range(STEPS):
        for d in range(8):

            @pl.when(exists(d))
            def _(t=t, d=d):
                halo_copy(t, d, False).wait_send()

    for n in range(3):
        each_forward(n, lambda n, d: forward_copy(n, d, False).wait_send())
    for r in range(1, XPEERS):
        for c in range(2):
            x_copy(r, c).wait_send()

    scale = 0.25 / lax.axis_size("src")

    def unpack(kind, n, tile):
        s, g = n // 2, n % 2
        for a in range(4):
            part = pltpu.roll(tile, (LANES - 32 * a) % LANES, 1) if a else tile
            kout[kind, 4 * g + a, pl.ds(8 * s, 8), :] = part[:, :32]

    @pl.when(half == 0)
    def _():
        x_total(0)
        z_copy(0).wait_recv()
        for n in range(4):
            unpack(0, n, (z_send[n] + z_land[n]) * scale)
        rest = jnp.where(xpos == XPEERS - 1, (z_send[4] + z_land[4]) * scale, 0.0)
        tail = jnp.logical_and(lane8 >= 30, lane8 < 32)
        for x in range(8):
            for s in range(2):
                tile = pltpu.roll(rest, (30 - 2 * (2 * x + s)) % LANES, 1)
                kout[1, x, pl.ds(8 * s, 8), :] = jnp.where(tail, tile, 0.0)[:, :32]

    @pl.when(half == 1)
    def _():
        x_total(1)
        z_copy(1).wait_recv()
        for kind in range(2):
            for n in range(4):
                m = 5 + 4 * kind + n
                unpack(kind, n, (z_send[m] + z_land[m]) * scale)

    kernels_copy = pltpu.make_async_copy(kout, kernels_out, out_sem.at[1])
    kernels_copy.start()

    @pl.when(half == 0)
    def _():
        z_copy(1).wait_send()

    @pl.when(half == 1)
    def _():
        z_copy(0).wait_send()

    final_copy.wait()
    kernels_copy.wait()


def body(adj_now, adj_later, forward_field, lame_first, shear, buoyancy, seafloor_depth, station_columns, station_traces):
    f32, bf16 = jnp.float32, jnp.bfloat16
    vmem, dma = pltpu.VMEM, pltpu.SemaphoreType.DMA
    stations = station_columns.shape[1]
    anywhere = pl.BlockSpec(memory_space=pltpu.HBM)
    rows = 10 * PITCH
    return pl.pallas_call(
        kernel,
        name="adjoint",
        out_shape=(
            jax.ShapeDtypeStruct((1, 3, 8, 16, 256), f32),
            jax.ShapeDtypeStruct((2, 8, 16, 32), f32),
        ),
        in_specs=[anywhere] * 9,
        out_specs=(anywhere, anywhere),
        scratch_shapes=[
            vmem((STEPS, 3, 2, rows, LANES), f32),
            vmem((3, 8, 16, 256), f32),
            vmem((3, 8, 16, 256), f32),
            vmem((3, 8, 16, 256), f32),
            vmem((STEPS, 3, 8, 16, 256), bf16),
            vmem((STEPS, 3, 2, rows, LANES), f32),
            vmem((2, STEPS, 3, 16, 256), bf16),
            vmem((2, STEPS, 3, 2, 8, LANES), bf16),
            vmem((2, STEPS, 3, 2, 8, LANES), bf16),
            vmem((STEPS, 2, 3, 2, 8, LANES), f32),
            vmem((STEPS, 2, 3, 2, 8, LANES), f32),
            vmem((STEPS, 4, 4, LANES), f32),
            vmem((STEPS, 4, 4, LANES), f32),
            vmem((8, 16, 256), f32),
            vmem((8, 16, 256), f32),
            vmem((8, 16, 256), f32),
            vmem((8, 16), jnp.int32),
            vmem((1, stations), jnp.int32),
            vmem((STEPS, 1, stations), f32),
            vmem((2, 8, 16, LANES), f32),
            vmem((2, 8, 16, LANES), f32),
            vmem((STEPS, 2, 8, 16, LANES), f32),
            vmem((8, 16, LANES), jnp.int32),
            vmem((2, 2, 8, 16, LANES), f32),
            vmem((XPEERS, PACKS, 8, LANES), f32),
            vmem((3, PACKS, 8, LANES), f32),
            vmem((PACKS, 8, LANES), f32),
            vmem((PACKS, 8, LANES), f32),
            vmem((2, 8, 16, 32), f32),
            dma((9,)),
            dma((2,)),
            dma((STEPS, 8)),
            dma((STEPS, 8)),
            dma((3, 4)),
            dma((3, 4)),
            dma((3, 2)),
            dma((3, 2)),
            dma,
            dma,
            pltpu.SemaphoreType.REGULAR,
        ],
        compiler_params=pltpu.CompilerParams(
            collective_id=0, has_side_effects=True, vmem_limit_bytes=24 << 20
        ),
    )(
        *(
            pltpu.with_memory_space_constraint(v, pltpu.HBM)
            for v in (
                adj_now, adj_later, forward_field, lame_first, shear, buoyancy, seafloor_depth,
                station_columns, jnp.transpose(station_traces, (1, 0, 2)),
            )
        )
    )


def solution(mesh):
    in_specs = (
        P("src", None, "tx", "ty", None),
        P("src", None, "tx", "ty", None),
        P("src", None, None, "tx", "ty", None),
        P("tx", "ty", None),
        P("tx", "ty", None),
        P("tx", "ty", None),
        P("tx", "ty"),
        P("src", None),
        P("src", None, None),
    )
    out_specs = (P("src", None, "tx", "ty", None), P(None, "tx", "ty", "src"))
    return jax.shard_map(body, mesh=mesh, in_specs=in_specs, out_specs=out_specs, check_vma=False)
```

```python
import functools

import jax
import jax.numpy as jnp
from jax import lax
from jax.experimental import pallas as pl
from jax.experimental.pallas import tpu as pltpu
from jax.sharding import PartitionSpec as P

STEPS = 3
TIME_SCALE = 0.04
MESH = pl.DeviceIdType.MESH
LANES = 128
PITCH = 32
FIRST = 8
XPEERS = 4
PACKS = 13
DIRS = ((-1, 0), (1, 0), (0, -1), (0, 1), (-1, -1), (-1, 1), (1, -1), (1, 1))


def opposite(d):
    return DIRS.index((-DIRS[d][0], -DIRS[d][1]))


def kernel(
    adj_now, adj_later, forward, lame, shear, buoyancy, seafloor, columns, traces,
    adj_out, kernels_out,
    u, now, prev, fin, fraw, fw, fx_land, fy_send, fy_land,
    y_send, y_land, c_send, c_land,
    p_lame, p_shear, p_buoy, p_sea, p_cols, p_traces,
    c_lap, c_div, q_add, sea_cols, acc, pack, x_land, z_send, z_land, kout,
    load_sem, out_sem, halo_send, halo_recv, fwd_send, fwd_recv, x_sem_s, x_sem_r, z_sem_s, z_sem_r, far_ready,
):
    tx, ty, src = lax.axis_index("tx"), lax.axis_index("ty"), lax.axis_index("src")
    ntx, nty = lax.axis_size("tx"), lax.axis_size("ty")
    half, xpos = src // XPEERS, lax.rem(src, XPEERS)

    def exists(d):
        dx, dy = DIRS[d]
        good = None
        for pos, step, count in ((tx, dx, ntx), (ty, dy, nty)):
            if step:
                here = (pos > 0) if step < 0 else (pos < count - 1)
                good = here if good is None else jnp.logical_and(good, here)
        return good

    def neighbour(d):
        dx, dy = DIRS[d]
        target = {}
        if dx:
            target["tx"] = tx + dx
        if dy:
            target["ty"] = ty + dy
        return target

    def src_peer(r):
        return {"src": half * XPEERS + lax.rem(xpos + r, XPEERS)}

    far = {"src": (1 - half) * XPEERS + xpos}

    loads = (
        (adj_now.at[0], now),
        (forward.at[0], fraw),
        (adj_later.at[0], prev),
        (lame, p_lame),
        (shear, p_shear),
        (buoyancy, p_buoy),
        (seafloor, p_sea),
        (columns, p_cols),
        (traces, p_traces),
    )
    copies = [pltpu.make_async_copy(a, b, load_sem.at[n]) for n, (a, b) in enumerate(loads)]
    copies[0].start()

    barrier = pltpu.get_barrier_semaphore()
    expected = XPEERS - 1 + half
    for d in range(8):
        there = exists(d)
        expected = expected + there.astype(jnp.int32)

        @pl.when(there)
        def _(d=d):
            pl.semaphore_signal(barrier, inc=1, device_id=neighbour(d), device_id_type=MESH)

    for r in range(1, XPEERS):
        pl.semaphore_signal(barrier, inc=1, device_id=src_peer(r), device_id_type=MESH)

    @pl.when(half == 0)
    def _():
        pl.semaphore_signal(barrier, inc=1, device_id=far, device_id_type=MESH)

    pl.semaphore_wait(barrier, expected)

    @pl.when(half == 1)
    def _():
        pl.semaphore_signal(far_ready, inc=1, device_id=far, device_id_type=MESH)


    def x_rows(t, plane):
        return u.at[t, :, :, pl.ds(plane * PITCH + FIRST, 16), :]

    def halo_source(t, d):
        if d == 0:
            return x_rows(t, 1)
        if d == 1:
            return x_rows(t, 8)
        if d < 4:
            return y_send.at[t, d - 2]
        return c_send.at[t, d - 4]

    def halo_target(t, d):
        if d == 0:
            return x_rows(t, 0)
        if d == 1:
            return x_rows(t, 9)
        if d < 4:
            return y_land.at[t, d - 2]
        return c_land.at[t, d - 4]

    def halo_copy(t, d, arrive):
        side = d if arrive else opposite(d)
        return pltpu.make_async_remote_copy(
            src_ref=halo_source(t, d),
            dst_ref=halo_target(t, side),
            send_sem=halo_send.at[t, d],
            recv_sem=halo_recv.at[t, side],
            device_id=neighbour(d),
            device_id_type=MESH,
        )

    def corner_row(d):
        dx, dy = DIRS[d]
        return (1 if dx < 0 else 8) * PITCH + (FIRST if dy < 0 else FIRST + 15)

    def start(t, directions):
        for d in directions:

            @pl.when(exists(d))
            def _(d=d):
                halo_copy(t, d, False).start()

    def send_corners(t):
        for d in range(4, 8):
            for k in range(2):
                for c in range(2):
                    row = corner_row(d)
                    c_send[t, d - 4, pl.ds(2 * k + c, 1), :] = u[t, k, c, pl.ds(row, 1), :]
        start(t, range(4, 8))

    def send_y(t):
        for k in range(3):
            for c in range(2):
                y_send[t, 0, k, c] = u[t, k, c, pl.ds(PITCH + FIRST, 8, stride=PITCH), :]
                y_send[t, 1, k, c] = u[t, k, c, pl.ds(PITCH + FIRST + 15, 8, stride=PITCH), :]
        start(t, range(2, 4))

    def receive_halo(t):
        for d in range(8):

            @pl.when(exists(d))
            def _(d=d):
                halo_copy(t, d, True).wait_recv()

        for k in range(3):
            for c in range(2):
                u[t, k, c, pl.ds(PITCH + FIRST - 1, 8, stride=PITCH), :] = y_land[t, 0, k, c]
                u[t, k, c, pl.ds(PITCH + FIRST + 16, 8, stride=PITCH), :] = y_land[t, 1, k, c]
        for d in range(4, 8):
            dx, dy = DIRS[d]
            row = (0 if dx < 0 else 9) * PITCH + (FIRST - 1 if dy < 0 else FIRST + 16)
            for k in range(2):
                for c in range(2):
                    u[t, k, c, pl.ds(row, 1), :] = c_land[t, d - 4, pl.ds(2 * k + c, 1), :]

    for d in range(2):

        @pl.when(exists(d))
        def _(d=d):
            side = opposite(d)
            for c in range(2):
                pltpu.make_async_remote_copy(
                    src_ref=adj_now.at[0, :, 7 * d, :, pl.ds(c * LANES, LANES)],
                    dst_ref=u.at[0, :, c, pl.ds((9 if side else 0) * PITCH + FIRST, 16), :],
                    send_sem=halo_send.at[0, d],
                    recv_sem=halo_recv.at[0, side],
                    device_id=neighbour(d),
                    device_id_type=MESH,
                ).start()

    for copy in copies[1:]:
        copy.start()

    def forward_copy(n, d, arrive):
        side = d if arrive else opposite(d)
        if n != 1:
            steps = pl.ds(0, 1) if n == 0 else pl.ds(1, STEPS - 1)
            source, target = fraw.at[steps, :, 7 * d], fx_land.at[side, steps]
        else:
            source, target = fy_send.at[d - 2], fy_land.at[side - 2]
        return pltpu.make_async_remote_copy(
            src_ref=source,
            dst_ref=target,
            send_sem=fwd_send.at[n, d],
            recv_sem=fwd_recv.at[n, side],
            device_id=neighbour(d),
            device_id_type=MESH,
        )

    def each_forward(n, act):
        for d in (2, 3) if n == 1 else (0, 1):

            @pl.when(exists(d))
            def _(d=d):
                act(n, d)

    lane = lax.broadcasted_iota(jnp.int32, (16, LANES), 1)
    is_first, is_last = lane == 0, lane == LANES - 1

    def shift_z(pair):
        a, b = pair
        ua, ub = pltpu.roll(a, LANES - 1, 1), pltpu.roll(b, LANES - 1, 1)
        da, db = pltpu.roll(a, 1, 1), pltpu.roll(b, 1, 1)
        above = (jnp.where(is_last, ub, ua), jnp.where(is_last, 0.0, ub))
        below = (jnp.where(is_first, 0.0, da), jnp.where(is_first, da, db))
        return above, below

    def diff_z(pair):
        above, below = shift_z(pair)
        return [above[c] - below[c] for c in range(2)]

    copies[0].wait()
    for k in range(3):
        for x in range(8):
            for c in range(2):
                rows = now[k, x, :, c * LANES : (c + 1) * LANES]
                u[0, k, c, pl.ds((x + 1) * PITCH + FIRST, 16), :] = rows
    send_corners(0)
    send_y(0)
    copies[1].wait()
    each_forward(0, lambda n, d: forward_copy(n, d, False).start())

    zero = jnp.zeros((16, LANES), jnp.float32)
    for d in range(2):

        @pl.when(jnp.logical_not(exists(d)))
        def _(d=d):
            plane = 0 if d == 0 else 9
            for t in range(STEPS):
                for k in range(3):
                    for c in range(2):
                        u[t, k, c, pl.ds(plane * PITCH + FIRST, 16), :] = zero
            fx_land[d] = jnp.zeros(fx_land.shape[1:], fx_land.dtype)

    for d in range(2, 4):

        @pl.when(jnp.logical_not(exists(d)))
        def _(d=d):
            for t in range(STEPS):
                y_land[t, d - 2] = jnp.zeros(y_land.shape[2:], jnp.float32)
            fy_land[d - 2] = jnp.zeros(fy_land.shape[1:], fy_land.dtype)

    for d in range(4, 8):

        @pl.when(jnp.logical_not(exists(d)))
        def _(d=d):
            for t in range(STEPS):
                c_land[t, d - 4] = jnp.zeros(c_land.shape[2:], jnp.float32)


    def widen(n, carry):
        t, k = n // 3, lax.rem(n, 3)
        for x in range(8):
            rows = fraw[t, k, x].astype(jnp.float32)
            for c in range(2):
                fw[t, k, c, pl.ds((x + 1) * PITCH + FIRST, 16), :] = rows[:, c * LANES : (c + 1) * LANES]
        for c in range(2):
            for side in range(2):
                row = PITCH + FIRST + 15 * side
                fy_send[side, t, k, c] = fw[t, k, c, pl.ds(row, 8, stride=PITCH), :].astype(fy_send.dtype)
        return carry

    lax.fori_loop(0, 3 * STEPS, widen, 0)
    each_forward(1, lambda n, d: forward_copy(n, d, False).start())

    for copy in copies[2:]:
        copy.wait()
    sublane = lax.broadcasted_iota(jnp.int32, (16, 16), 0)
    sublane_lane = lax.broadcasted_iota(jnp.int32, (16, 16), 1)
    stations = p_cols.shape[1]
    y_of = lax.broadcasted_iota(jnp.int32, (16, stations), 0)
    total_y = 16 * nty

    def coefficients(x, carry):
        depth_row = jnp.broadcast_to(p_sea[pl.ds(x, 1), :].astype(jnp.float32), (16, 16))
        depth = jnp.sum(jnp.where(sublane == sublane_lane, depth_row, 0.0), axis=1, keepdims=True)
        depth = jnp.broadcast_to(depth, (16, LANES)).astype(jnp.int32)
        sea_cols[x] = depth
        column = (tx * 8 + x) * total_y + ty * 16 + y_of
        hit = jnp.broadcast_to(p_cols[...], (16, stations)) == column
        amps = []
        for t in range(STEPS):
            amp = jnp.broadcast_to(p_traces[t], (16, stations))
            amp = jnp.sum(jnp.where(hit, amp, 0.0), axis=1, keepdims=True)
            amps.append(jnp.broadcast_to(amp, (16, LANES)))
        for c in range(2):
            zs = slice(c * LANES, (c + 1) * LANES)
            scaled = TIME_SCALE * p_buoy[x, :, zs]
            level = lane + c * LANES
            mu = jnp.where(level >= depth, p_shear[x, :, zs], 0.0)
            c_lap[c, x] = scaled * mu
            c_div[c, x] = scaled * (p_lame[x, :, zs] + mu)
            for t in range(STEPS):
                q_add[t, c, x] = jnp.where(level == depth, scaled * amps[t], 0.0)
        return carry

    lax.fori_loop(0, 8, coefficients, 0)

    def step(t, first, count, stride):
        def row(i, carry):
            x = first + i * stride
            base = (x + 1) * PITCH + FIRST

            def at(k, c, dx, dy):
                return u[t, k, c, pl.ds(base + dx * PITCH + dy, 16), :]

            both = range(2)
            centre = [[at(k, c, 0, 0) for c in both] for k in range(3)]
            gx, gy, fresh = [], [], []
            lap, second = [], []
            for k in range(3):
                xp, xm = [at(k, c, 1, 0) for c in both], [at(k, c, -1, 0) for c in both]
                yp, ym = [at(k, c, 0, 1) for c in both], [at(k, c, 0, -1) for c in both]
                zp, zm = shift_z(centre[k])
                gx.append([xp[c] - xm[c] for c in both])
                gy.append([yp[c] - ym[c] for c in both])
                sums = [[a[c] + b[c] for c in both] for a, b in ((xp, xm), (yp, ym), (zp, zm))]
                lap.append([sums[0][c] + sums[1][c] + sums[2][c] - 6.0 * centre[k][c] for c in both])
                second.append([sums[k][c] - 2.0 * centre[k][c] for c in both])

            def cross(k):
                return [
                    (at(k, c, 1, 1) - at(k, c, -1, 1)) - (at(k, c, 1, -1) - at(k, c, -1, -1)) for c in both
                ]

            cross_0, cross_1 = cross(0), cross(1)
            dz_gx2, dz_gy2 = diff_z(gx[2]), diff_z(gy[2])
            dz_mix = diff_z([gx[0][c] + gy[1][c] for c in both])
            mixed = [
                [cross_1[c] + dz_gx2[c] for c in both],
                [cross_0[c] + dz_gy2[c] for c in both],
                dz_mix,
            ]
            for k in range(3):
                for c in both:
                    if t == 0:
                        old = prev[k, x, :, c * LANES : (c + 1) * LANES]
                    else:
                        old = u[t - 1, k, c, pl.ds(base, 16), :]
                    new = (
                        (2.0 * centre[k][c] - old)
                        + c_lap[c, x] * lap[k][c]
                        + c_div[c, x] * (second[k][c] + 0.25 * mixed[k][c])
                    )
                    if k == 2:
                        new = new + q_add[t, c, x]
                    if t < STEPS - 1:
                        u[t + 1, k, c, pl.ds(base, 16), :] = new
                    else:
                        fin[k, x, :, c * LANES : (c + 1) * LANES] = new
            return carry

        lax.fori_loop(0, count, row, 0, unroll=2)

    def receive_forward(t):
        for n in ((0, 1), (2,), ())[t]:
            each_forward(n, lambda n, d: forward_copy(n, d, True).wait_recv())
        for k in range(3):
            for side in range(2):
                plane = 9 * side
                rows = fx_land[side, t, k].astype(jnp.float32)
                for c in range(2):
                    fw[t, k, c, pl.ds(plane * PITCH + FIRST, 16), :] = rows[:, c * LANES : (c + 1) * LANES]
                    row = PITCH + (FIRST - 1 if side == 0 else FIRST + 16)
                    fw[t, k, c, pl.ds(row, 8, stride=PITCH), :] = fy_land[side, t, k, c].astype(jnp.float32)

    def diff_z_half(a, b, c):
        if c == 0:
            above = jnp.where(is_last, pltpu.roll(b, LANES - 1, 1), pltpu.roll(a, LANES - 1, 1))
            below = jnp.where(is_first, 0.0, pltpu.roll(a, 1, 1))
        else:
            above = jnp.where(is_last, 0.0, pltpu.roll(b, LANES - 1, 1))
            below = jnp.where(is_first, pltpu.roll(a, 1, 1), pltpu.roll(b, 1, 1))
        return above - below

    def accumulate(t, both=(0, 1)):
        def row(x, carry):
            base = (x + 1) * PITCH + FIRST

            def gradient(ref, k):
                at = lambda c, dx, dy: ref[t, k, c, pl.ds(base + dx * PITCH + dy, 16), :]
                g_x = {c: at(c, 1, 0) - at(c, -1, 0) for c in both}
                g_y = {c: at(c, 0, 1) - at(c, 0, -1) for c in both}
                pair = [at(c, 0, 0) for c in range(2)]
                if len(both) == 2:
                    g_z = diff_z(pair)
                else:
                    g_z = {both[0]: diff_z_half(*pair, both[0])}
                return g_x, g_y, g_z

            mu = div_u = div_f = None
            for k in range(3):
                gu, gf = gradient(u, k), gradient(fw, k)
                for d in range(3):
                    term = {c: gu[d][c] * gf[d][c] for c in both}
                    mu = term if mu is None else {c: mu[c] + term[c] for c in both}
                div_u = gu[k] if div_u is None else {c: div_u[c] + gu[k][c] for c in both}
                div_f = gf[k] if div_f is None else {c: div_f[c] + gf[k][c] for c in both}
            for c in both:
                lam = div_u[c] * div_f[c]
                if t == 0:
                    acc[0, c, x], acc[1, c, x] = lam, mu[c]
                else:
                    acc[0, c, x] = acc[0, c, x] + lam
                    acc[1, c, x] = acc[1, c, x] + mu[c]
            return carry

        lax.fori_loop(0, 8, row, 0, unroll=2)

    receive_halo(0)
    for t in range(STEPS - 1):
        step(t, 0, 2, 7)
        start(t + 1, range(2))
        send_corners(t + 1)
        step(t, 1, 6, 1)
        send_y(t + 1)
        if t == 0:
            each_forward(2, lambda n, d: forward_copy(n, d, False).start())
        receive_forward(t)
        accumulate(t)
        receive_halo(t + 1)
    lane8 = lax.broadcasted_iota(jnp.int32, (8, LANES), 1)
    even = lax.rem(lane8 // 32, 2) == 0
    low = lane8 < 64

    def quarters(v):
        w = []
        for a, b in ((v[0], v[1]), (v[2], v[3])):
            w.append(
                (
                    jnp.where(even, a, pltpu.roll(b, 32, 1)),
                    jnp.where(even, pltpu.roll(a, 96, 1), b),
                )
            )
        out = [None] * 4
        for odd in range(2):
            a, b = w[0][odd], w[1][odd]
            out[odd] = jnp.where(low, a, pltpu.roll(b, 64, 1))
            out[2 + odd] = jnp.where(low, pltpu.roll(a, 64, 1), b)
        return out

    def masked_mu(c, x, ys):
        return jnp.where(lane8 + c * LANES >= sea_cols[x, ys], acc[1, c, x, ys], 0.0)

    parts = ((0, 5), (5, 8))

    def fill(c):
        for s in range(2):
            ys = pl.ds(8 * s, 8)
            for g in range(2):
                n = parts[c][0] + 2 * s + g
                for q, tile in enumerate(quarters([acc[0, c, 4 * g + a, ys] for a in range(4)])):
                    pack[q, n] = tile
                if c == 1:
                    for q, tile in enumerate(quarters([masked_mu(1, 4 * g + a, ys) for a in range(4)])):
                        pack[q, n + 4] = tile
        if c == 0:
            rest = None
            for x in range(8):
                for s in range(2):
                    tile = masked_mu(0, x, pl.ds(8 * s, 8))
                    tile = pltpu.roll(tile, (2 * (2 * x + s) + 2) % LANES, 1)
                    rest = tile if rest is None else rest + tile
            for q in range(XPEERS):
                pack[q, 4] = rest

    def x_copy(r, c):
        rows = pl.ds(*parts[c])
        return pltpu.make_async_remote_copy(
            src_ref=pack.at[lax.rem(xpos + r, XPEERS), rows],
            dst_ref=x_land.at[r - 1, rows],
            send_sem=x_sem_s.at[r - 1, c],
            recv_sem=x_sem_r.at[r - 1, c],
            device_id=src_peer(r),
            device_id_type=MESH,
        )

    def x_total(c):
        for r in (1, 3, 2):
            x_copy(r, c).wait_recv()
        for n in range(parts[c][0], sum(parts[c])):
            z_send[n] = pack[xpos, n] + x_land[0, n] + x_land[1, n] + x_land[2, n]

    def z_copy(c):
        rows = pl.ds(*parts[c])
        return pltpu.make_async_remote_copy(
            src_ref=z_send.at[rows],
            dst_ref=z_land.at[rows],
            send_sem=z_sem_s,
            recv_sem=z_sem_r,
            device_id=far,
            device_id_type=MESH,
        )

    receive_forward(STEPS - 1)
    for mine in range(2):

        @pl.when(half == mine)
        def _(mine=mine):
            for c in (1 - mine, mine):
                accumulate(STEPS - 1, (c,))
                fill(c)
                for r in (2, 1, 3):
                    x_copy(r, c).start()
            x_total(1 - mine)
            if mine == 0:
                pl.semaphore_wait(far_ready, 1)
            z_copy(1 - mine).start()

    step(STEPS - 1, 0, 8, 1)
    final_copy = pltpu.make_async_copy(fin, adj_out.at[0], out_sem.at[0])
    final_copy.start()

    for t in range(STEPS):
        for d in range(8):

            @pl.when(exists(d))
            def _(t=t, d=d):
                halo_copy(t, d, False).wait_send()

    for n in range(3):
        each_forward(n, lambda n, d: forward_copy(n, d, False).wait_send())
    for r in range(1, XPEERS):
        for c in range(2):
            x_copy(r, c).wait_send()

    scale = 0.25 / lax.axis_size("src")

    def kernels_copy(kind):
        return pltpu.make_async_copy(kout.at[kind], kernels_out.at[kind], out_sem.at[1 + kind])

    def unpack(kind, n, tile):
        s, g = n // 2, n % 2
        for a in range(4):
            part = pltpu.roll(tile, (LANES - 32 * a) % LANES, 1) if a else tile
            kout[kind, 4 * g + a, pl.ds(8 * s, 8), :] = part[:, :32]

    @pl.when(half == 0)
    def _():
        x_total(0)
        z_copy(0).wait_recv()
        for n in range(4):
            unpack(0, n, (z_send[n] + z_land[n]) * scale)
        kernels_copy(0).start()
        rest = jnp.where(xpos == XPEERS - 1, (z_send[4] + z_land[4]) * scale, 0.0)
        tail = jnp.logical_and(lane8 >= 30, lane8 < 32)
        for x in range(8):
            for s in range(2):
                tile = pltpu.roll(rest, (30 - 2 * (2 * x + s)) % LANES, 1)
                kout[1, x, pl.ds(8 * s, 8), :] = jnp.where(tail, tile, 0.0)[:, :32]
        kernels_copy(1).start()

    @pl.when(half == 1)
    def _():
        x_total(1)
        z_copy(1).wait_recv()
        for kind in range(2):
            for n in range(4):
                m = 5 + 4 * kind + n
                unpack(kind, n, (z_send[m] + z_land[m]) * scale)
            kernels_copy(kind).start()


    @pl.when(half == 0)
    def _():
        z_copy(1).wait_send()

    @pl.when(half == 1)
    def _():
        z_copy(0).wait_send()

    final_copy.wait()
    for kind in range(2):
        kernels_copy(kind).wait()


def body(adj_now, adj_later, forward_field, lame_first, shear, buoyancy, seafloor_depth, station_columns, station_traces):
    f32, bf16 = jnp.float32, jnp.bfloat16
    vmem, dma = pltpu.VMEM, pltpu.SemaphoreType.DMA
    stations = station_columns.shape[1]
    anywhere = pl.BlockSpec(memory_space=pltpu.HBM)
    rows = 10 * PITCH
    return pl.pallas_call(
        kernel,
        name="adjoint",
        out_shape=(
            jax.ShapeDtypeStruct((1, 3, 8, 16, 256), f32),
            jax.ShapeDtypeStruct((2, 8, 16, 32), f32),
        ),
        in_specs=[anywhere] * 9,
        out_specs=(anywhere, anywhere),
        scratch_shapes=[
            vmem((STEPS, 3, 2, rows, LANES), f32),
            vmem((3, 8, 16, 256), f32),
            vmem((3, 8, 16, 256), f32),
            vmem((3, 8, 16, 256), f32),
            vmem((STEPS, 3, 8, 16, 256), bf16),
            vmem((STEPS, 3, 2, rows, LANES), f32),
            vmem((2, STEPS, 3, 16, 256), bf16),
            vmem((2, STEPS, 3, 2, 8, LANES), bf16),
            vmem((2, STEPS, 3, 2, 8, LANES), bf16),
            vmem((STEPS, 2, 3, 2, 8, LANES), f32),
            vmem((STEPS, 2, 3, 2, 8, LANES), f32),
            vmem((STEPS, 4, 4, LANES), f32),
            vmem((STEPS, 4, 4, LANES), f32),
            vmem((8, 16, 256), f32),
            vmem((8, 16, 256), f32),
            vmem((8, 16, 256), f32),
            vmem((8, 16), jnp.int32),
            vmem((1, stations), jnp.int32),
            vmem((STEPS, 1, stations), f32),
            vmem((2, 8, 16, LANES), f32),
            vmem((2, 8, 16, LANES), f32),
            vmem((STEPS, 2, 8, 16, LANES), f32),
            vmem((8, 16, LANES), jnp.int32),
            vmem((2, 2, 8, 16, LANES), f32),
            vmem((XPEERS, PACKS, 8, LANES), f32),
            vmem((3, PACKS, 8, LANES), f32),
            vmem((PACKS, 8, LANES), f32),
            vmem((PACKS, 8, LANES), f32),
            vmem((2, 8, 16, 32), f32),
            dma((9,)),
            dma((3,)),
            dma((STEPS, 8)),
            dma((STEPS, 8)),
            dma((3, 4)),
            dma((3, 4)),
            dma((3, 2)),
            dma((3, 2)),
            dma,
            dma,
            pltpu.SemaphoreType.REGULAR,
        ],
        compiler_params=pltpu.CompilerParams(
            collective_id=0, has_side_effects=True, vmem_limit_bytes=24 << 20
        ),
    )(
        *(
            pltpu.with_memory_space_constraint(v, pltpu.HBM)
            for v in (
                adj_now, adj_later, forward_field, lame_first, shear, buoyancy, seafloor_depth,
                station_columns, jnp.transpose(station_traces, (1, 0, 2)),
            )
        )
    )


def solution(mesh):
    in_specs = (
        P("src", None, "tx", "ty", None),
        P("src", None, "tx", "ty", None),
        P("src", None, None, "tx", "ty", None),
        P("tx", "ty", None),
        P("tx", "ty", None),
        P("tx", "ty", None),
        P("tx", "ty"),
        P("src", None),
        P("src", None, None),
    )
    out_specs = (P("src", None, "tx", "ty", None), P(None, "tx", "ty", "src"))
    return jax.shard_map(body, mesh=mesh, in_specs=in_specs, out_specs=out_specs, check_vma=False)
```
